32 devices in a mesh: blk: 16 (over z, y, x), col: 2 (over core).
Axes of the slice: x: 2, y: 2, z: 4, core: 2. Of those that a mesh axis runs over, the one named last changes fastest.
Arguments:
- trial: bfloat16 [32768, 128], P(('blk', 'col')), may hold values from -6 to 6
- omega: float32 [32768], P(('blk', 'col')), may hold values from 0.5 to 6
- table: bfloat16 [64, 128, 128], replicated, may hold values from -0.0625 to 0.0625
- block_type: int32 [256, 72], P(('blk', 'col')), may hold values from 0 to 63
- cycle_offset: int32 [256, 72], P(('blk', 'col')), may hold values from -4 to 4
- source_block: int32 [256, 72], P(('blk', 'col')), may hold values from 0 to 7
Outputs:
- sigma: bfloat16 [32768, 128], P(('blk', 'col'))
- projected: float32 [128, 128], replicated
- basis: float32 [32768, 128], P(('blk', 'col'))
The draws below stay inside these ranges and needn't reach their ends.
All inputs are finite; a program needn't handle non-finite values.
Results may differ from the reference program's by a relative error of at most 0.006.
Values may be sent and summed in bfloat16 or wider, within the bound.
A program may use at most 64 MiB of HBM per device.

```python
import jax
import jax.numpy as jnp
from jax import lax

K = 128
BLOCK = 128
RB_DEV = 8
NB = 72
NTYPE = 64
REACH = 4
RBLK = 256
PAIRS = 32768
N_BLK = 16
N_COL = 2


def draw_omega(key, part):
    uniform_part = jax.random.uniform(key, (PAIRS,), jnp.float32)
    ramp = 3.0 ** (jnp.arange(PAIRS, dtype=jnp.float32) / PAIRS)
    base = 0.5 * 4.0 ** uniform_part
    return base * ramp


def touch_ends(array, stream_key, least, top_value):
    extent = array.shape
    place = [jax.random.randint(jax.random.fold_in(stream_key, axis), (), 0, extent[axis]) for axis in range(len(extent))]
    array = array.at[tuple(place)].set(least)
    longest = extent.index(max(extent))
    place[longest] = (place[longest] + 1) % extent[longest]
    return array.at[tuple(place)].set(top_value)


def steps_of(own_key, shape, pieces, low, largest):
    gain = 1.0
    for axis_at, shards_of in pieces:
        draws = jax.random.uniform(jax.random.fold_in(jax.random.fold_in(own_key, 6), axis_at), (shards_of,), jnp.float32, low / len(pieces), largest / len(pieces))
        gain = gain * jnp.repeat(jnp.exp(draws), shape[axis_at] // shards_of).reshape((-1,) + (1,) * (len(shape) - 1 - axis_at))
    return gain


def normal_values(own_key, extent, scale, limit, pieces=(), kind=jnp.bfloat16):
    result = scale * jax.random.normal(own_key, extent, jnp.float32)
    if pieces:
        result = result * steps_of(own_key, extent, pieces, -0.22, 0.18)
    return jnp.clip(result, -limit, limit).astype(kind)


def setup_inputs(seed: int = 0) -> dict:
    key_of = jax.random.split(jax.random.key(seed), 7)
    return {
        "trial": normal_values(key_of[0], (PAIRS, K), 1.0, 6.0, ((0, 32),)),
        "omega": draw_omega(jax.random.fold_in(key_of[6], 71), 0),
        "table": normal_values(key_of[2], (NTYPE, BLOCK, BLOCK), (BLOCK * NB) ** -0.5, 0.0625),
        "block_type": touch_ends(jax.random.randint(key_of[3], (RBLK, NB), 0, NTYPE), jax.random.fold_in(key_of[3], 1), 0, NTYPE - 1).astype(jnp.int32),
        "cycle_offset": touch_ends(jax.random.randint(key_of[4], (RBLK, NB), 0 - REACH, REACH + 1), jax.random.fold_in(key_of[4], 1), 0 - REACH, REACH).astype(jnp.int32),
        "source_block": touch_ends(jax.random.randint(key_of[5], (RBLK, NB), 0, RB_DEV), jax.random.fold_in(key_of[5], 1), 0, RB_DEV - 1).astype(jnp.int32),
    }


def reference(trial, omega, table, block_type, cycle_offset, source_block):
    groups = N_BLK * N_COL
    trial_groups = trial.reshape(groups, RB_DEV, BLOCK, K)
    trial_five = trial.reshape(N_BLK, N_COL, RB_DEV, BLOCK, K)
    omega_groups = omega.reshape(groups, RB_DEV, BLOCK)
    type_groups = block_type.reshape(groups, RB_DEV, NB)
    cycle_groups = cycle_offset.reshape(groups, RB_DEV, NB)
    source_groups = source_block.reshape(groups, RB_DEV, NB)
    device_ids = jnp.arange(groups, dtype=jnp.int32)

    def one_group(operands):
        device_id, own_rows, energy, kinds, cycles, chosen = operands
        slab_id = device_id // N_COL
        column_id = device_id % N_COL
        far_slab = ((slab_id + cycles) % N_BLK).astype(jnp.int32)
        sources = trial_five[far_slab, column_id, chosen]
        coeffs = table[kinds]
        coupled = jnp.einsum('rjab,rjbk->rak', coeffs.astype(jnp.float32), sources.astype(jnp.float32))
        return (coupled + energy[:, :, None] * own_rows.astype(jnp.float32)).astype(jnp.bfloat16)
    sigma = lax.map(one_group, (device_ids, trial_groups, omega_groups, type_groups, cycle_groups, source_groups))
    sigma = sigma.reshape(PAIRS, K)
    highest = lax.Precision.HIGHEST
    sigma_full = sigma.astype(jnp.float32)
    trial_full = trial.astype(jnp.float32)
    projected = jnp.dot(trial_full.T, sigma_full, precision=highest) / PAIRS
    residual = sigma_full - jnp.dot(trial_full, projected, precision=highest)
    gram = jnp.dot(residual.T, residual, precision=highest) / PAIRS
    lower = jnp.linalg.cholesky(gram)
    inverse = jax.scipy.linalg.solve_triangular(lower, jnp.eye(K, dtype=jnp.float32), lower=True)
    basis = jnp.dot(residual, inverse.T, precision=highest)
    return (sigma, projected, basis)
```

```python
import functools

import jax
import jax.numpy as jnp
from jax import lax
from jax.experimental import pallas as pl
from jax.experimental.pallas import tpu as pltpu
from jax.sharding import PartitionSpec as P

REACH = 4
MESH = pl.DeviceIdType.MESH
HIGHEST = lax.Precision.HIGHEST
PARTS = 4


def wrap(index, count):
    return lax.rem(index + count, count)


def spread(count, mine, source, target, send, recv, place):
    copies = []
    for step in range(1, count):
        peer = wrap(mine + step, count)
        copy = pltpu.make_async_remote_copy(
            src_ref=source(peer),
            dst_ref=target(step),
            send_sem=send.at[step - 1],
            recv_sem=recv.at[step - 1],
            device_id=place(peer),
            device_id_type=MESH,
        )
        copy.start()
        copies.append(copy)
    return copies


def rows_at(index, size):
    return pl.ds(pl.multiple_of(index * size, 8), size)


def couple_kernel(
    n_blk, n_col, near,
    kinds_ref, cycle_ref, source_ref, trial_hbm, omega_hbm, table_hbm,
    sigma_ref, sums_ref,
    table_ref, slabs, across, omega_ref,
    own_part, own_got, own_ring, own_total,
    part, got, ring, total,
    local_sems, g_send, g_recv,
    o_send, o_recv, oz_send, oz_recv, oa_send, oa_recv,
    r_send, r_recv, z_send, z_recv, a_send, a_recv,
):
    blocks, pair_block, vec_count = trial_hbm.shape
    per_row = kinds_ref.shape[1]
    me_b = lax.axis_index("blk")
    me_c = lax.axis_index("col")

    group = near * n_col
    far = n_blk // near
    low = lax.rem(me_b, near)
    high = me_b // near
    mine = low * n_col + me_c

    def near_id(index):
        return (high * near + index // n_col, lax.rem(index, n_col))

    def far_id(index):
        return (index * near + low, me_c)

    keep_own = pltpu.make_async_copy(trial_hbm, slabs.at[REACH], local_sems.at[0])
    keep_own.start()
    load_omega = pltpu.make_async_copy(omega_hbm, omega_ref, local_sems.at[1])
    load_omega.start()
    load_table = pltpu.make_async_copy(table_hbm, table_ref, local_sems.at[2])
    load_table.start()

    x = lax.rem(low, 2)
    y = low // 2
    ahead = wrap(me_b - REACH + 2 * REACH * y, n_blk)
    behind = wrap(me_b + REACH - 2 * REACH * y, n_blk)
    side_x = me_b + 1 - 2 * x
    side_y = me_b + 2 - 4 * y

    barrier = pltpu.get_barrier_semaphore()
    for step in range(1, far):
        pl.semaphore_signal(
            barrier, inc=1, device_id=far_id(wrap(high + step, far)), device_id_type=MESH
        )
    for step in range(1, group):
        pl.semaphore_signal(
            barrier, inc=1, device_id=near_id(wrap(mine + step, group)), device_id_type=MESH
        )
    pl.semaphore_wait(barrier, group - 1 + far - 1)

    span = blocks // PARTS

    def message(number, h, source, slot, target):
        rows_of = pl.ds(h * span, span)
        return pltpu.make_async_remote_copy(
            src_ref=trial_hbm.at[rows_of] if source is None else slabs.at[source, rows_of],
            dst_ref=slabs.at[slot, rows_of],
            send_sem=g_send.at[number, h],
            recv_sem=g_recv.at[number, h],
            device_id=(target, me_c),
            device_id_type=MESH,
        )

    parts = range(PARTS)
    first_z = [message(0, h, None, 8 - 8 * y, ahead) for h in parts]
    second_z = [message(1, h, None, 8 * y, behind) for h in parts]
    own_x = [message(2, h, None, 3 + 2 * x, side_x) for h in parts]
    own_y = [message(3, h, None, 2 + 4 * y, side_y) for h in parts]
    pass_y = [message(4, h, 5 - 2 * x, 3 - 2 * x + 4 * y, side_y) for h in parts]
    far_x = [message(5, h, 8 - 8 * x, 7 - 6 * x, side_x) for h in parts]
    far_y = [message(6, h, 8 - 8 * y, 6 - 4 * y, side_y) for h in parts]
    pass_x = [message(7, h, 2 + 4 * y, 1 + 4 * y + 2 * x, side_x) for h in parts]

    for h in parts:
        first_z[h].start()
        own_x[h].start()
        if h < PARTS // 2:
            own_y[h].start()

    keep_own.wait()
    own = slabs[REACH].reshape(blocks * pair_block, vec_count)
    across[...] = own.T
    own_part[...] = jnp.dot(across[...], own, preferred_element_type=jnp.float32)

    for h in parts:
        first_z[h].wait_recv()
        far_y[h].start()

        @pl.when(x == y)
        def _():
            far_x[h].start()

    for h in parts:
        second_z[h].start()
        if h >= PARTS // 2:
            own_y[h].start()
    for h in parts:
        far_y[h].wait_recv()
        pass_x[h].start()
        own_x[h].wait_recv()
        pass_y[h].start()
    for h in parts:
        second_z[h].wait_recv()

        @pl.when(x != y)
        def _():
            far_x[h].start()

    load_omega.wait()
    load_table.wait()
    for h in parts:
        own_y[h].wait_recv()
        pass_y[h].wait_recv()
        far_x[h].wait_recv()
        pass_x[h].wait_recv()

    def scatter(source, target, send, recv):
        size = target.shape[1]
        return spread(
            group, mine, lambda peer: source.at[rows_at(peer, size)],
            lambda step: target.at[step - 1], send, recv, near_id,
        )

    def across_far(copies, source, target, place, send, recv):
        size = target.shape[1]
        piece = source[rows_at(mine, size), :]
        for step, copy in enumerate(copies):
            copy.wait()
            piece = piece + target[step]
        place[high] = piece
        return spread(
            far, high, lambda peer: place.at[high], lambda step: place.at[high],
            send, recv, far_id,
        )

    def gather(copies, source, target, send, recv):
        for copy in copies:
            copy.wait()
        piece = source[0]
        for index in range(1, far):
            piece = piece + source[index]
        place = rows_at(mine, source.shape[1])
        target[place, :] = piece
        return spread(
            group, mine, lambda peer: target.at[place], lambda step: target.at[place],
            send, recv, near_id,
        )

    chunk = max(size for size in range(1, 9) if per_row % size == 0)
    row_id = lax.broadcasted_iota(jnp.int32, (pair_block, pair_block), 0)
    lane_id = lax.broadcasted_iota(jnp.int32, (pair_block, pair_block), 1)
    own_copies = scatter(own_part, own_got, o_send, o_recv)
    sums = None
    for r in range(blocks):
        energy = jnp.broadcast_to(omega_ref[r : r + 1, :], (pair_block, pair_block))
        column = jnp.sum(jnp.where(row_id == lane_id, energy, 0.0), axis=1, keepdims=True)
        acc = column * slabs[REACH, r].astype(jnp.float32)
        for start in range(0, per_row, chunk):
            coeffs = []
            sources = []
            for j in range(start, start + chunk):
                coeffs.append(table_ref[kinds_ref[r, j]])
                sources.append(slabs[cycle_ref[r, j] + REACH, source_ref[r, j]])
            acc = acc + jnp.dot(
                jnp.concatenate(coeffs, axis=1),
                jnp.concatenate(sources, axis=0),
                preferred_element_type=jnp.float32,
            )
        sigma_ref[r * pair_block : (r + 1) * pair_block, :] = acc.astype(jnp.bfloat16)
        if r % 2 == 1:
            place = slice((r - 1) * pair_block, (r + 1) * pair_block)
            sigma = sigma_ref[place, :]
            both = jnp.concatenate([across[:, place], sigma.T], axis=0)
            term = jnp.dot(both, sigma, preferred_element_type=jnp.float32)
            sums = term if sums is None else sums + term
    part[...] = sums

    copies = scatter(part, got, r_send, r_recv)
    own_copies = across_far(own_copies, own_part, own_got, own_ring, oz_send, oz_recv)
    for sent in (first_z, second_z, own_x, own_y, pass_y, far_x, far_y, pass_x):
        for h in parts:
            sent[h].wait_send()
    copies = across_far(copies, part, got, ring, z_send, z_recv)
    own_copies = gather(own_copies, own_ring, own_total, oa_send, oa_recv)
    copies = gather(copies, ring, total, a_send, a_recv)
    for copy in own_copies:
        copy.wait()
    sums_ref[0:vec_count, :] = own_total[...]
    for copy in copies:
        copy.wait()
    sums_ref[vec_count:, :] = total[...]


def split_three(value):
    high = value.astype(jnp.bfloat16)
    rest = value - high.astype(jnp.float32)
    middle = rest.astype(jnp.bfloat16)
    low = (rest - middle.astype(jnp.float32)).astype(jnp.bfloat16)
    return high, middle, low


def inverse_factor(gram):
    size = gram.shape[0]
    count = size // 8
    tiles = [gram[8 * t : 8 * t + 8, :] for t in range(count)]
    lane = lax.broadcasted_iota(jnp.int32, (8, size), 1)
    sub = lax.broadcasted_iota(jnp.int32, (8, size), 0)

    def spread_row(tile, k):
        return jnp.broadcast_to(tile[k : k + 1, :], (8, size))

    def spread_columns(tile, panel):
        return [
            jnp.broadcast_to(tile[:, 8 * panel + k : 8 * panel + k + 1], (8, size))
            for k in range(8)
        ]

    for panel in range(count):
        tile = tiles[panel]
        columns = spread_columns(tile, panel)
        later_rows = []
        factors = []
        for k in range(8):
            here = lane == 8 * panel + k
            reciprocal = 1.0 / spread_row(columns[k], k)
            scaled = jnp.where(here, 1.0, spread_row(tile, k)) * reciprocal
            later_rows.append(
                jnp.where((lane > 8 * panel + k) & (lane < 8 * panel + 8), 0.0, scaled)
            )
            factors.append({m: spread_row(columns[m], k) * reciprocal for m in range(k + 1, 8)})
            below = sub > k
            lead = jnp.where(below, columns[k], 0.0)
            tile = jnp.where(here & below, 0.0, tile) - lead * scaled
            for m in range(k + 1, 8):
                columns[m] = columns[m] - lead * factors[k][m]
        tiles[panel] = tile
        for t in range(panel + 1, count):
            tile = tiles[t]
            columns = spread_columns(tile, panel)
            tile = jnp.where((lane >= 8 * panel) & (lane < 8 * panel + 8), 0.0, tile)
            for k in range(8):
                tile = tile - columns[k] * later_rows[k]
                for m in range(k + 1, 8):
                    columns[m] = columns[m] - columns[k] * factors[k][m]
            tiles[t] = tile
    inverse = []
    for t in range(size // 8):
        diagonal = lane == sub + 8 * t
        pivots = jnp.sum(jnp.where(diagonal, tiles[t], 0.0), axis=1, keepdims=True)
        unit = jnp.where(diagonal, 1.0, jnp.where(lane < sub + 8 * t, tiles[t], 0.0))
        inverse.append(unit / jnp.sqrt(pivots))
    return jnp.concatenate(inverse, axis=0)


def basis_kernel(
    total_rows, sums_ref, trial_ref, coupled_ref, sigma_ref, projected_ref, basis_ref
):
    size = sums_ref.shape[1]
    scale = 1.0 / total_rows
    overlap = sums_ref[0:size, :] * scale
    projected = sums_ref[size : 2 * size, :] * scale
    projected_ref[...] = projected
    square = sums_ref[2 * size : 3 * size, :] * scale
    row = lax.broadcasted_iota(jnp.int32, (size, size), 0)
    lane = lax.broadcasted_iota(jnp.int32, (size, size), 1)
    middle = jnp.where(row == lane, 2.0, 0.0) - overlap
    folded = jnp.dot(middle, projected, precision=HIGHEST, preferred_element_type=jnp.float32)
    gram = square - lax.dot_general(
        projected, folded, (((0,), (0,)), ((), ())),
        precision=HIGHEST, preferred_element_type=jnp.float32,
    )
    inverse = inverse_factor(gram)
    upper = inverse.T
    pulled = jnp.dot(projected, upper, precision=HIGHEST, preferred_element_type=jnp.float32)
    weights = jnp.concatenate([upper, 0.0 - pulled], axis=0)
    coupled = coupled_ref[...]
    sigma_ref[...] = coupled
    both = jnp.concatenate([coupled, trial_ref[...]], axis=1)
    result = None
    for term in reversed(split_three(weights)):
        product = jnp.dot(both, term, preferred_element_type=jnp.float32)
        result = product if result is None else result + product
    basis_ref[...] = result


def on_device(n_blk, n_col, trial, omega, table, block_type, cycle_offset, source_block):
    row_count, vec_count = trial.shape
    pair_block = table.shape[1]
    blocks = row_count // pair_block
    rows = 2 * vec_count
    near = max(size for size in (4, 2, 1) if n_blk % size == 0)
    group = near * n_col
    far = n_blk // near
    rows = 2 * vec_count
    piece = rows // group
    own_piece = vec_count // group
    vmem = pl.BlockSpec(memory_space=pltpu.VMEM)
    smem = pl.BlockSpec(memory_space=pltpu.SMEM)
    hbm = pl.BlockSpec(memory_space=pltpu.HBM)
    dma = pltpu.SemaphoreType.DMA
    coupled, sums = pl.pallas_call(
        functools.partial(couple_kernel, n_blk, n_col, near),
        out_shape=(
            jax.ShapeDtypeStruct((row_count, vec_count), jnp.bfloat16),
            jax.ShapeDtypeStruct((3 * vec_count, vec_count), jnp.float32),
        ),
        in_specs=[smem, smem, smem, hbm, hbm, hbm],
        out_specs=(vmem, vmem),
        scratch_shapes=[
            pltpu.VMEM(table.shape, jnp.bfloat16),
            pltpu.VMEM((2 * REACH + 1, blocks, pair_block, vec_count), jnp.bfloat16),
            pltpu.VMEM((vec_count, row_count), jnp.bfloat16),
            pltpu.VMEM((blocks, pair_block), jnp.float32),
            pltpu.VMEM((vec_count, vec_count), jnp.float32),
            pltpu.VMEM((group - 1, own_piece, vec_count), jnp.float32),
            pltpu.VMEM((far, own_piece, vec_count), jnp.float32),
            pltpu.VMEM((vec_count, vec_count), jnp.float32),
            pltpu.VMEM((rows, vec_count), jnp.float32),
            pltpu.VMEM((group - 1, piece, vec_count), jnp.float32),
            pltpu.VMEM((far, piece, vec_count), jnp.float32),
            pltpu.VMEM((rows, vec_count), jnp.float32),
            dma((3,)),
            dma((8, PARTS)),
            dma((8, PARTS)),
            dma((group - 1,)),
            dma((group - 1,)),
            dma((far - 1,)),
            dma((far - 1,)),
            dma((group - 1,)),
            dma((group - 1,)),
            dma((group - 1,)),
            dma((group - 1,)),
            dma((far - 1,)),
            dma((far - 1,)),
            dma((group - 1,)),
            dma((group - 1,)),
        ],
        compiler_params=pltpu.CompilerParams(
            collective_id=0, has_side_effects=True, vmem_limit_bytes=60 << 20
        ),
        name="couple",
    )(
        block_type,
        cycle_offset,
        source_block,
        trial.reshape(blocks, pair_block, vec_count),
        omega.reshape(blocks, pair_block),
        table,
    )
    sigma, projected, basis = pl.pallas_call(
        functools.partial(basis_kernel, row_count * n_blk * n_col),
        out_shape=(
            jax.ShapeDtypeStruct((row_count, vec_count), jnp.bfloat16),
            jax.ShapeDtypeStruct((vec_count, vec_count), jnp.float32),
            jax.ShapeDtypeStruct((row_count, vec_count), jnp.float32),
        ),
        in_specs=[vmem] * 3,
        out_specs=(vmem, vmem, vmem),
        compiler_params=pltpu.CompilerParams(vmem_limit_bytes=60 << 20),
        name="basis",
    )(sums, trial, coupled)
    return (sigma, projected, basis)


def solution(mesh):
    placed = (
        P(("blk", "col"), None),
        P(("blk", "col")),
        P(),
        P(("blk", "col"), None),
        P(("blk", "col"), None),
        P(("blk", "col"), None),
    )
    return jax.shard_map(
        functools.partial(on_device, mesh.shape["blk"], mesh.shape["col"]),
        mesh=mesh,
        in_specs=placed,
        out_specs=(P(("blk", "col"), None), P(), P(("blk", "col"), None)),
        check_vma=False,
    )
```

```python
import functools

import jax
import jax.numpy as jnp
from jax import lax
from jax.experimental import pallas as pl
from jax.experimental.pallas import tpu as pltpu
from jax.sharding import PartitionSpec as P

REACH = 4
MESH = pl.DeviceIdType.MESH
HIGHEST = lax.Precision.HIGHEST
PARTS = 4
HALF = PARTS // 2


def wrap(index, count):
    return lax.rem(index + count, count)


def spread(count, mine, source, target, send, recv, place):
    copies = []
    for step in range(1, count):
        peer = wrap(mine + step, count)
        copy = pltpu.make_async_remote_copy(
            src_ref=source(peer),
            dst_ref=target(step),
            send_sem=send.at[step - 1],
            recv_sem=recv.at[step - 1],
            device_id=place(peer),
            device_id_type=MESH,
        )
        copy.start()
        copies.append(copy)
    return copies


def rows_at(index, size):
    return pl.ds(pl.multiple_of(index * size, 8), size)


def couple_kernel(
    n_blk, n_col, near,
    kinds_ref, cycle_ref, source_ref, trial_hbm, omega_hbm, table_hbm,
    sigma_ref, sums_ref,
    table_ref, turned_ref, first_half, second_half, own_ref, across, omega_ref, acc_ref,
    own_part, own_got, own_ring, own_total,
    part, got, ring, total,
    local_sems, g_send, g_recv,
    o_send, o_recv, oz_send, oz_recv, oa_send, oa_recv,
    r_send, r_recv, z_send, z_recv, a_send, a_recv,
):
    blocks, pair_block, vec_count = trial_hbm.shape
    per_row = kinds_ref.shape[1]
    me_b = lax.axis_index("blk")
    me_c = lax.axis_index("col")

    group = near * n_col
    far = n_blk // near
    low = lax.rem(me_b, near)
    high = me_b // near
    mine = low * n_col + me_c

    def near_id(index):
        return (high * near + index // n_col, lax.rem(index, n_col))

    def far_id(index):
        return (index * near + low, me_c)

    middle = pair_block // 2
    halves = (first_half, second_half)
    keep_half = []
    for which in range(2):
        copy = pltpu.make_async_copy(
            trial_hbm.at[:, pl.ds(which * middle, middle)],
            halves[which].at[REACH],
            local_sems.at[3 + which],
        )
        copy.start()
        keep_half.append(copy)
    keep_own = pltpu.make_async_copy(trial_hbm, own_ref, local_sems.at[0])
    keep_own.start()
    load_omega = pltpu.make_async_copy(omega_hbm, omega_ref, local_sems.at[1])
    load_omega.start()
    load_table = pltpu.make_async_copy(table_hbm, table_ref, local_sems.at[2])
    load_table.start()

    x = lax.rem(low, 2)
    y = low // 2
    ahead = wrap(me_b - REACH + 2 * REACH * y, n_blk)
    behind = wrap(me_b + REACH - 2 * REACH * y, n_blk)
    side_x = me_b + 1 - 2 * x
    side_y = me_b + 2 - 4 * y

    barrier = pltpu.get_barrier_semaphore()
    for step in range(1, far):
        pl.semaphore_signal(
            barrier, inc=1, device_id=far_id(wrap(high + step, far)), device_id_type=MESH
        )
    for step in range(1, group):
        pl.semaphore_signal(
            barrier, inc=1, device_id=near_id(wrap(mine + step, group)), device_id_type=MESH
        )
    pl.semaphore_wait(barrier, group - 1 + far - 1)

    span = blocks // HALF

    def message(number, h, source, slot, target):
        which = h // HALF
        blocks_of = pl.ds((h % HALF) * span, span)
        rows_of = pl.ds(which * middle, middle)
        slabs = halves[which]
        return pltpu.make_async_remote_copy(
            src_ref=trial_hbm.at[blocks_of, rows_of] if source is None else slabs.at[source, blocks_of],
            dst_ref=slabs.at[slot, blocks_of],
            send_sem=g_send.at[number, h],
            recv_sem=g_recv.at[number, h],
            device_id=(target, me_c),
            device_id_type=MESH,
        )

    parts = range(PARTS)
    first_z = [message(0, h, None, 8 - 8 * y, ahead) for h in parts]
    second_z = [message(1, h, None, 8 * y, behind) for h in parts]
    own_x = [message(2, h, None, 3 + 2 * x, side_x) for h in parts]
    own_y = [message(3, h, None, 2 + 4 * y, side_y) for h in parts]
    pass_y = [message(4, h, 5 - 2 * x, 3 - 2 * x + 4 * y, side_y) for h in parts]
    far_x = [message(5, h, 8 - 8 * x, 7 - 6 * x, side_x) for h in parts]
    far_y = [message(6, h, 8 - 8 * y, 6 - 4 * y, side_y) for h in parts]
    pass_x = [message(7, h, 2 + 4 * y, 1 + 4 * y + 2 * x, side_x) for h in parts]

    early = range(HALF)
    late = range(HALF, PARTS)

    def relay_first(h):
        first_z[h].wait_recv()
        far_y[h].start()

        @pl.when(x == y)
        def _():
            far_x[h].start()

    def relay_own(h):
        own_x[h].wait_recv()
        pass_y[h].start()

    def relay_second(h):
        second_z[h].wait_recv()

        @pl.when(x != y)
        def _():
            far_x[h].start()

    def relay_far(h):
        far_y[h].wait_recv()
        pass_x[h].start()

    def arrived(h):
        own_y[h].wait_recv()
        pass_y[h].wait_recv()
        far_x[h].wait_recv()
        pass_x[h].wait_recv()

    for h in early:
        first_z[h].start()
        own_x[h].start()
        own_y[h].start()
    for h in early:
        second_z[h].start()

    load_table.wait()

    def turn(index, carry):
        turned_ref[index] = jnp.roll(table_ref[index], middle, axis=1)
        return carry

    lax.fori_loop(0, table_ref.shape[0], turn, 0, unroll=8)
    keep_own.wait()
    own = own_ref[...].reshape(blocks * pair_block, vec_count)
    across[...] = own.T
    own_part[...] = jnp.dot(across[...], own, preferred_element_type=jnp.float32)
    load_omega.wait()

    for h in early:
        relay_first(h)
        first_z[HALF + h].start()
    for h in late:
        own_x[h].start()
        second_z[h].start()
    for h in early:
        relay_own(h)
    for h in early:
        relay_second(h)
    for h in early:
        relay_far(h)
    for h in late:
        relay_first(h)
    for h in late:
        own_y[h].start()
    for h in late:
        relay_second(h)
    for h in late:
        relay_own(h)
    for h in early:
        arrived(h)
    keep_half[0].wait()
    for h in late:
        relay_far(h)

    def scatter(source, target, send, recv):
        size = target.shape[1]
        return spread(
            group, mine, lambda peer: source.at[rows_at(peer, size)],
            lambda step: target.at[step - 1], send, recv, near_id,
        )

    def across_far(copies, source, target, place, send, recv):
        size = target.shape[1]
        piece = source[rows_at(mine, size), :]
        for step, copy in enumerate(copies):
            copy.wait()
            piece = piece + target[step]
        place[high] = piece
        return spread(
            far, high, lambda peer: place.at[high], lambda step: place.at[high],
            send, recv, far_id,
        )

    def gather(copies, source, target, send, recv):
        for copy in copies:
            copy.wait()
        piece = source[0]
        for index in range(1, far):
            piece = piece + source[index]
        place = rows_at(mine, source.shape[1])
        target[place, :] = piece
        return spread(
            group, mine, lambda peer: target.at[place], lambda step: target.at[place],
            send, recv, near_id,
        )

    pairs = per_row // 2
    chunk = max(size for size in range(1, 9) if pairs % size == 0)
    row_id = lax.broadcasted_iota(jnp.int32, (pair_block, pair_block), 0)
    lane_id = lax.broadcasted_iota(jnp.int32, (pair_block, pair_block), 1)
    left_id = lax.broadcasted_iota(jnp.int32, table_ref.shape[1:], 1) < middle

    def products(r, which, acc):
        left, right = (table_ref, turned_ref) if which == 0 else (turned_ref, table_ref)
        slabs = halves[which]
        for start in range(0, pairs, chunk):
            coeffs = []
            sources = []
            for pair in range(start, start + chunk):
                j = 2 * pair
                coeffs.append(jnp.where(left_id, left[kinds_ref[r, j]], right[kinds_ref[r, j + 1]]))
                sources.append(slabs[cycle_ref[r, j] + REACH, source_ref[r, j]])
                sources.append(slabs[cycle_ref[r, j + 1] + REACH, source_ref[r, j + 1]])
            acc = acc + jnp.dot(
                jnp.concatenate(coeffs, axis=1),
                jnp.concatenate(sources, axis=0),
                preferred_element_type=jnp.float32,
            )
        return acc

    for r in range(blocks):
        energy = jnp.broadcast_to(omega_ref[r : r + 1, :], (pair_block, pair_block))
        column = jnp.sum(jnp.where(row_id == lane_id, energy, 0.0), axis=1, keepdims=True)
        acc_ref[r] = products(r, 0, column * own_ref[r].astype(jnp.float32))

    for h in late:
        arrived(h)
    keep_half[1].wait()
    own_copies = scatter(own_part, own_got, o_send, o_recv)
    sums = None
    for r in range(blocks):
        acc = products(r, 1, acc_ref[r])
        sigma_ref[r * pair_block : (r + 1) * pair_block, :] = acc.astype(jnp.bfloat16)
        if r % 2 == 1:
            place = slice((r - 1) * pair_block, (r + 1) * pair_block)
            sigma = sigma_ref[place, :]
            both = jnp.concatenate([across[:, place], sigma.T], axis=0)
            term = jnp.dot(both, sigma, preferred_element_type=jnp.float32)
            sums = term if sums is None else sums + term
    part[...] = sums

    copies = scatter(part, got, r_send, r_recv)
    own_copies = across_far(own_copies, own_part, own_got, own_ring, oz_send, oz_recv)
    for sent in (first_z, second_z, own_x, own_y, pass_y, far_x, far_y, pass_x):
        for h in parts:
            sent[h].wait_send()
    copies = across_far(copies, part, got, ring, z_send, z_recv)
    own_copies = gather(own_copies, own_ring, own_total, oa_send, oa_recv)
    copies = gather(copies, ring, total, a_send, a_recv)
    for copy in own_copies:
        copy.wait()
    sums_ref[0:vec_count, :] = own_total[...]
    for copy in copies:
        copy.wait()
    sums_ref[vec_count:, :] = total[...]


def split_three(value):
    high = value.astype(jnp.bfloat16)
    rest = value - high.astype(jnp.float32)
    middle = rest.astype(jnp.bfloat16)
    low = (rest - middle.astype(jnp.float32)).astype(jnp.bfloat16)
    return high, middle, low


def inverse_factor(gram):
    size = gram.shape[0]
    count = size // 8
    tiles = [gram[8 * t : 8 * t + 8, :] for t in range(count)]
    lane = lax.broadcasted_iota(jnp.int32, (8, size), 1)
    sub = lax.broadcasted_iota(jnp.int32, (8, size), 0)

    def spread_row(tile, k):
        return jnp.broadcast_to(tile[k : k + 1, :], (8, size))

    def spread_columns(tile, panel):
        return [
            jnp.broadcast_to(tile[:, 8 * panel + k : 8 * panel + k + 1], (8, size))
            for k in range(8)
        ]

    for panel in range(count):
        tile = tiles[panel]
        columns = spread_columns(tile, panel)
        later_rows = []
        factors = []
        for k in range(8):
            here = lane == 8 * panel + k
            reciprocal = 1.0 / spread_row(columns[k], k)
            scaled = jnp.where(here, 1.0, spread_row(tile, k)) * reciprocal
            later_rows.append(
                jnp.where((lane > 8 * panel + k) & (lane < 8 * panel + 8), 0.0, scaled)
            )
            factors.append({m: spread_row(columns[m], k) * reciprocal for m in range(k + 1, 8)})
            below = sub > k
            lead = jnp.where(below, columns[k], 0.0)
            tile = jnp.where(here & below, 0.0, tile) - lead * scaled
            for m in range(k + 1, 8):
                columns[m] = columns[m] - lead * factors[k][m]
        tiles[panel] = tile
        for t in range(panel + 1, count):
            tile = tiles[t]
            columns = spread_columns(tile, panel)
            tile = jnp.where((lane >= 8 * panel) & (lane < 8 * panel + 8), 0.0, tile)
            for k in range(8):
                tile = tile - columns[k] * later_rows[k]
                for m in range(k + 1, 8):
                    columns[m] = columns[m] - columns[k] * factors[k][m]
            tiles[t] = tile
    inverse = []
    for t in range(size // 8):
        diagonal = lane == sub + 8 * t
        pivots = jnp.sum(jnp.where(diagonal, tiles[t], 0.0), axis=1, keepdims=True)
        unit = jnp.where(diagonal, 1.0, jnp.where(lane < sub + 8 * t, tiles[t], 0.0))
        inverse.append(unit / jnp.sqrt(pivots))
    return jnp.concatenate(inverse, axis=0)


def basis_kernel(
    total_rows, sums_ref, trial_ref, coupled_ref, sigma_ref, projected_ref, basis_ref
):
    size = sums_ref.shape[1]
    scale = 1.0 / total_rows
    overlap = sums_ref[0:size, :] * scale
    projected = sums_ref[size : 2 * size, :] * scale
    projected_ref[...] = projected
    square = sums_ref[2 * size : 3 * size, :] * scale
    row = lax.broadcasted_iota(jnp.int32, (size, size), 0)
    lane = lax.broadcasted_iota(jnp.int32, (size, size), 1)
    middle = jnp.where(row == lane, 2.0, 0.0) - overlap
    folded = jnp.dot(middle, projected, precision=HIGHEST, preferred_element_type=jnp.float32)
    gram = square - lax.dot_general(
        projected, folded, (((0,), (0,)), ((), ())),
        precision=HIGHEST, preferred_element_type=jnp.float32,
    )
    inverse = inverse_factor(gram)
    upper = inverse.T
    pulled = jnp.dot(projected, upper, precision=HIGHEST, preferred_element_type=jnp.float32)
    weights = jnp.concatenate([upper, 0.0 - pulled], axis=0)
    coupled = coupled_ref[...]
    sigma_ref[...] = coupled
    both = jnp.concatenate([coupled, trial_ref[...]], axis=1)
    result = None
    for term in reversed(split_three(weights)):
        product = jnp.dot(both, term, preferred_element_type=jnp.float32)
        result = product if result is None else result + product
    basis_ref[...] = result


def on_device(n_blk, n_col, trial, omega, table, block_type, cycle_offset, source_block):
    row_count, vec_count = trial.shape
    pair_block = table.shape[1]
    blocks = row_count // pair_block
    rows = 2 * vec_count
    near = max(size for size in (4, 2, 1) if n_blk % size == 0)
    group = near * n_col
    far = n_blk // near
    rows = 2 * vec_count
    piece = rows // group
    own_piece = vec_count // group
    vmem = pl.BlockSpec(memory_space=pltpu.VMEM)
    smem = pl.BlockSpec(memory_space=pltpu.SMEM)
    hbm = pl.BlockSpec(memory_space=pltpu.HBM)
    dma = pltpu.SemaphoreType.DMA
    coupled, sums = pl.pallas_call(
        functools.partial(couple_kernel, n_blk, n_col, near),
        out_shape=(
            jax.ShapeDtypeStruct((row_count, vec_count), jnp.bfloat16),
            jax.ShapeDtypeStruct((3 * vec_count, vec_count), jnp.float32),
        ),
        in_specs=[smem, smem, smem, hbm, hbm, hbm],
        out_specs=(vmem, vmem),
        scratch_shapes=[
            pltpu.VMEM(table.shape, jnp.bfloat16),
            pltpu.VMEM(table.shape, jnp.bfloat16),
            pltpu.VMEM((2 * REACH + 1, blocks, pair_block // 2, vec_count), jnp.bfloat16),
            pltpu.VMEM((2 * REACH + 1, blocks, pair_block // 2, vec_count), jnp.bfloat16),
            pltpu.VMEM((blocks, pair_block, vec_count), jnp.bfloat16),
            pltpu.VMEM((vec_count, row_count), jnp.bfloat16),
            pltpu.VMEM((blocks, pair_block), jnp.float32),
            pltpu.VMEM((blocks, pair_block, vec_count), jnp.float32),
            pltpu.VMEM((vec_count, vec_count), jnp.float32),
            pltpu.VMEM((group - 1, own_piece, vec_count), jnp.float32),
            pltpu.VMEM((far, own_piece, vec_count), jnp.float32),
            pltpu.VMEM((vec_count, vec_count), jnp.float32),
            pltpu.VMEM((rows, vec_count), jnp.float32),
            pltpu.VMEM((group - 1, piece, vec_count), jnp.float32),
            pltpu.VMEM((far, piece, vec_count), jnp.float32),
            pltpu.VMEM((rows, vec_count), jnp.float32),
            dma((5,)),
            dma((8, PARTS)),
            dma((8, PARTS)),
            dma((group - 1,)),
            dma((group - 1,)),
            dma((far - 1,)),
            dma((far - 1,)),
            dma((group - 1,)),
            dma((group - 1,)),
            dma((group - 1,)),
            dma((group - 1,)),
            dma((far - 1,)),
            dma((far - 1,)),
            dma((group - 1,)),
            dma((group - 1,)),
        ],
        compiler_params=pltpu.CompilerParams(
            collective_id=0, has_side_effects=True, vmem_limit_bytes=60 << 20
        ),
        name="couple",
    )(
        block_type,
        cycle_offset,
        source_block,
        trial.reshape(blocks, pair_block, vec_count),
        omega.reshape(blocks, pair_block),
        table,
    )
    sigma, projected, basis = pl.pallas_call(
        functools.partial(basis_kernel, row_count * n_blk * n_col),
        out_shape=(
            jax.ShapeDtypeStruct((row_count, vec_count), jnp.bfloat16),
            jax.ShapeDtypeStruct((vec_count, vec_count), jnp.float32),
            jax.ShapeDtypeStruct((row_count, vec_count), jnp.float32),
        ),
        in_specs=[vmem] * 3,
        out_specs=(vmem, vmem, vmem),
        compiler_params=pltpu.CompilerParams(vmem_limit_bytes=60 << 20),
        name="basis",
    )(sums, trial, coupled)
    return (sigma, projected, basis)


def solution(mesh):
    placed = (
        P(("blk", "col"), None),
        P(("blk", "col")),
        P(),
        P(("blk", "col"), None),
        P(("blk", "col"), None),
        P(("blk", "col"), None),
    )
    return jax.shard_map(
        functools.partial(on_device, mesh.shape["blk"], mesh.shape["col"]),
        mesh=mesh,
        in_specs=placed,
        out_specs=(P(("blk", "col"), None), P(), P(("blk", "col"), None)),
        check_vma=False,
    )
```

```python
import functools

import jax
import jax.numpy as jnp
from jax import lax
from jax.experimental import pallas as pl
from jax.experimental.pallas import tpu as pltpu
from jax.sharding import PartitionSpec as P

REACH = 4
MESH = pl.DeviceIdType.MESH
HIGHEST = lax.Precision.HIGHEST
PARTS = 4
HALF = PARTS // 2


def wrap(index, count):
    return lax.rem(index + count, count)


def spread(count, mine, source, target, send, recv, place):
    copies = []
    for step in range(1, count):
        peer = wrap(mine + step, count)
        copy = pltpu.make_async_remote_copy(
            src_ref=source(peer),
            dst_ref=target(step),
            send_sem=send.at[step - 1],
            recv_sem=recv.at[step - 1],
            device_id=place(peer),
            device_id_type=MESH,
        )
        copy.start()
        copies.append(copy)
    return copies


def rows_at(index, size):
    return pl.ds(pl.multiple_of(index * size, 8), size)


def couple_kernel(
    n_blk, n_col, near,
    kinds_ref, cycle_ref, source_ref, trial_hbm, omega_hbm, table_hbm,
    sigma_ref, sums_ref,
    table_ref, turned_ref, first_half, second_half, own_ref, across, omega_ref, acc_ref,
    own_part, own_got, own_ring, own_total,
    part, got, ring, total,
    local_sems, g_send, g_recv,
    o_send, o_recv, oz_send, oz_recv, oa_send, oa_recv,
    r_send, r_recv, z_send, z_recv, a_send, a_recv,
):
    blocks, pair_block, vec_count = trial_hbm.shape
    per_row = kinds_ref.shape[1]
    me_b = lax.axis_index("blk")
    me_c = lax.axis_index("col")

    group = near * n_col
    far = n_blk // near
    low = lax.rem(me_b, near)
    high = me_b // near
    mine = low * n_col + me_c

    def near_id(index):
        return (high * near + index // n_col, lax.rem(index, n_col))

    def far_id(index):
        return (index * near + low, me_c)

    middle = pair_block // 2
    halves = (first_half, second_half)
    keep_half = []
    for which in range(2):
        copy = pltpu.make_async_copy(
            trial_hbm.at[:, pl.ds(which * middle, middle)],
            halves[which].at[REACH],
            local_sems.at[3 + which],
        )
        copy.start()
        keep_half.append(copy)
    keep_own = pltpu.make_async_copy(trial_hbm, own_ref, local_sems.at[0])
    keep_own.start()
    load_omega = pltpu.make_async_copy(omega_hbm, omega_ref, local_sems.at[1])
    load_omega.start()
    load_table = pltpu.make_async_copy(table_hbm, table_ref, local_sems.at[2])
    load_table.start()

    x = lax.rem(low, 2)
    y = low // 2
    ahead = wrap(me_b - REACH + 2 * REACH * y, n_blk)
    behind = wrap(me_b + REACH - 2 * REACH * y, n_blk)
    side_x = me_b + 1 - 2 * x
    side_y = me_b + 2 - 4 * y

    barrier = pltpu.get_barrier_semaphore()
    for step in range(1, far):
        pl.semaphore_signal(
            barrier, inc=1, device_id=far_id(wrap(high + step, far)), device_id_type=MESH
        )
    for step in range(1, group):
        pl.semaphore_signal(
            barrier, inc=1, device_id=near_id(wrap(mine + step, group)), device_id_type=MESH
        )
    pl.semaphore_wait(barrier, group - 1 + far - 1)

    span = blocks // HALF

    def message(number, h, source, slot, target):
        which = h // HALF
        blocks_of = pl.ds((h % HALF) * span, span)
        rows_of = pl.ds(which * middle, middle)
        slabs = halves[which]
        return pltpu.make_async_remote_copy(
            src_ref=trial_hbm.at[blocks_of, rows_of] if source is None else slabs.at[source, blocks_of],
            dst_ref=slabs.at[slot, blocks_of],
            send_sem=g_send.at[number, h],
            recv_sem=g_recv.at[number, h],
            device_id=(target, me_c),
            device_id_type=MESH,
        )

    parts = range(PARTS)
    first_z = [message(0, h, None, 8 - 8 * y, ahead) for h in parts]
    second_z = [message(1, h, None, 8 * y, behind) for h in parts]
    own_x = [message(2, h, None, 3 + 2 * x, side_x) for h in parts]
    own_y = [message(3, h, None, 2 + 4 * y, side_y) for h in parts]
    pass_y = [message(4, h, 5 - 2 * x, 3 - 2 * x + 4 * y, side_y) for h in parts]
    far_x = [message(5, h, 8 - 8 * x, 7 - 6 * x, side_x) for h in parts]
    far_y = [message(6, h, 8 - 8 * y, 6 - 4 * y, side_y) for h in parts]
    pass_x = [message(7, h, 2 + 4 * y, 1 + 4 * y + 2 * x, side_x) for h in parts]

    early = range(HALF)
    late = range(HALF, PARTS)

    def relay_first(h):
        first_z[h].wait_recv()
        far_y[h].start()

        @pl.when(x == y)
        def _():
            far_x[h].start()

    def relay_own(h):
        own_x[h].wait_recv()
        pass_y[h].start()

    def relay_second(h):
        second_z[h].wait_recv()

        @pl.when(x != y)
        def _():
            far_x[h].start()

    def relay_far(h):
        far_y[h].wait_recv()
        pass_x[h].start()

    def arrived(h):
        own_y[h].wait_recv()
        pass_y[h].wait_recv()
        far_x[h].wait_recv()
        pass_x[h].wait_recv()

    for h in early:
        first_z[h].start()
        own_x[h].start()
        own_y[h].start()
    for h in early:
        second_z[h].start()

    load_table.wait()

    def turn(index, carry):
        turned_ref[index] = jnp.roll(table_ref[index], middle, axis=1)
        return carry

    lax.fori_loop(0, table_ref.shape[0], turn, 0, unroll=8)
    keep_own.wait()
    own = own_ref[...].reshape(blocks * pair_block, vec_count)
    across[...] = own.T
    own_part[...] = jnp.dot(across[...], own, preferred_element_type=jnp.float32)
    load_omega.wait()

    for h in early:
        relay_first(h)
        first_z[HALF + h].start()
    for h in late:
        own_x[h].start()
        second_z[h].start()
    for h in early:
        relay_own(h)
    for h in early:
        relay_second(h)
    for h in early:
        relay_far(h)
    for h in late:
        relay_first(h)
    for h in late:
        own_y[h].start()
    for h in late:
        relay_second(h)
    for h in late:
        relay_own(h)
    for h in early:
        arrived(h)
    keep_half[0].wait()
    for h in late:
        relay_far(h)

    def scatter(source, target, send, recv):
        size = target.shape[1]
        return spread(
            group, mine, lambda peer: source.at[rows_at(peer, size)],
            lambda step: target.at[step - 1], send, recv, near_id,
        )

    def across_far(copies, source, target, place, send, recv):
        size = target.shape[1]
        piece = source[rows_at(mine, size), :]
        for step, copy in enumerate(copies):
            copy.wait()
            piece = piece + target[step]
        place[high] = piece
        return spread(
            far, high, lambda peer: place.at[high], lambda step: place.at[high],
            send, recv, far_id,
        )

    def gather(copies, source, target, send, recv):
        for copy in copies:
            copy.wait()
        piece = source[0]
        for index in range(1, far):
            piece = piece + source[index]
        place = rows_at(mine, source.shape[1])
        target[place, :] = piece
        return spread(
            group, mine, lambda peer: target.at[place], lambda step: target.at[place],
            send, recv, near_id,
        )

    pairs = per_row // 2
    chunk = max(size for size in range(1, 9) if pairs % size == 0)
    row_id = lax.broadcasted_iota(jnp.int32, (pair_block, pair_block), 0)
    lane_id = lax.broadcasted_iota(jnp.int32, (pair_block, pair_block), 1)
    left_id = lax.broadcasted_iota(jnp.int32, table_ref.shape[1:], 1) < middle

    def products(r, which, acc):
        left, right = (table_ref, turned_ref) if which == 0 else (turned_ref, table_ref)
        slabs = halves[which]
        for start in range(0, pairs, chunk):
            coeffs = []
            sources = []
            for pair in range(start, start + chunk):
                j = 2 * pair
                coeffs.append(jnp.where(left_id, left[kinds_ref[r, j]], right[kinds_ref[r, j + 1]]))
                sources.append(slabs[cycle_ref[r, j] + REACH, source_ref[r, j]])
                sources.append(slabs[cycle_ref[r, j + 1] + REACH, source_ref[r, j + 1]])
            acc = acc + jnp.dot(
                jnp.concatenate(coeffs, axis=1),
                jnp.concatenate(sources, axis=0),
                preferred_element_type=jnp.float32,
            )
        return acc

    for r in range(blocks):
        energy = jnp.broadcast_to(omega_ref[r : r + 1, :], (pair_block, pair_block))
        column = jnp.sum(jnp.where(row_id == lane_id, energy, 0.0), axis=1, keepdims=True)
        acc_ref[r] = products(r, 0, column * own_ref[r].astype(jnp.float32))

    for h in late:
        arrived(h)
    keep_half[1].wait()
    own_copies = scatter(own_part, own_got, o_send, o_recv)
    sums = None
    for r in range(blocks):
        acc = products(r, 1, acc_ref[r])
        sigma_ref[r * pair_block : (r + 1) * pair_block, :] = acc.astype(jnp.bfloat16)
        if r % 2 == 1:
            place = slice((r - 1) * pair_block, (r + 1) * pair_block)
            sigma = sigma_ref[place, :]
            both = jnp.concatenate([across[:, place], sigma.T], axis=0)
            term = jnp.dot(both, sigma, preferred_element_type=jnp.float32)
            sums = term if sums is None else sums + term
    part[...] = sums

    copies = scatter(part, got, r_send, r_recv)
    own_copies = across_far(own_copies, own_part, own_got, own_ring, oz_send, oz_recv)
    for sent in (first_z, second_z, own_x, own_y, pass_y, far_x, far_y, pass_x):
        for h in parts:
            sent[h].wait_send()
    copies = across_far(copies, part, got, ring, z_send, z_recv)
    own_copies = gather(own_copies, own_ring, own_total, oa_send, oa_recv)
    copies = gather(copies, ring, total, a_send, a_recv)
    for copy in own_copies:
        copy.wait()
    sums_ref[0:vec_count, :] = own_total[...]
    for copy in copies:
        copy.wait()
    sums_ref[vec_count:, :] = total[...]


def split_three(value):
    high = value.astype(jnp.bfloat16)
    rest = value - high.astype(jnp.float32)
    middle = rest.astype(jnp.bfloat16)
    low = (rest - middle.astype(jnp.float32)).astype(jnp.bfloat16)
    return high, middle, low


def inverse_factor(gram):
    size = gram.shape[0]
    count = size // 8
    tiles = [gram[8 * t : 8 * t + 8, :] for t in range(count)]
    lane = lax.broadcasted_iota(jnp.int32, (8, size), 1)
    sub = lax.broadcasted_iota(jnp.int32, (8, size), 0)

    def spread_row(tile, k):
        return jnp.broadcast_to(tile[k : k + 1, :], (8, size))

    def spread_columns(tile, panel):
        return [
            jnp.broadcast_to(tile[:, 8 * panel + k : 8 * panel + k + 1], (8, size))
            for k in range(8)
        ]

    columns = spread_columns(tiles[0], 0)
    for panel in range(count):
        tile = tiles[panel]
        full = tile
        follows = panel + 1 < count
        if follows:
            below = spread_columns(tiles[panel + 1], panel)
            ahead = spread_columns(tiles[panel + 1], panel + 1)
        for k in range(0, 8, 2):
            n = k + 1
            corner = spread_row(columns[k], k)
            side = spread_row(columns[n], k)
            other = spread_row(columns[n], n)
            first = 1.0 / corner
            second = corner * (1.0 / (corner * other - side * side))
            row_k = {m: spread_row(columns[m], k) * first for m in range(n, 8)}
            row_n = {
                m: (spread_row(columns[m], n) - side * row_k[m]) * second for m in range(n + 1, 8)
            }
            lead_k = jnp.where(sub == k, 0.0, columns[k])
            lead_n = jnp.where(sub == n, 0.0, columns[n] - lead_k * row_k[n])
            lead_n = jnp.where(sub == k, row_k[n], lead_n)
            for m in range(n + 1, 8):
                column = jnp.where(sub == k, row_k[m], columns[m] - lead_k * row_k[m])
                columns[m] = jnp.where(sub == n, row_n[m], column - lead_n * row_n[m])
            for lead, reciprocal, at in ((lead_k, first, k), (lead_n, second, n)):
                here = lane == 8 * panel + at
                scaled = jnp.where(here, 1.0, spread_row(tile, at)) * reciprocal
                cleared = jnp.where(here & (sub > at), 0.0, tile)
                tile = cleared - jnp.where(sub > at, lead, 0.0) * scaled
                full = jnp.where(sub == at, scaled, jnp.where(here, 0.0, full) - lead * scaled)
            if follows:
                below[n] = below[n] - below[k] * row_k[n]
                for m in range(n + 1, 8):
                    below[m] = below[m] - below[k] * row_k[m] - below[n] * row_n[m]
                scaled_k = below[k] * first
                scaled_n = below[n] * second
                for m in range(8):
                    ahead[m] = (
                        ahead[m]
                        - below[k] * spread_row(scaled_k, m)
                        - below[n] * spread_row(scaled_n, m)
                    )
        tiles[panel] = tile
        rows = [spread_row(full, k) for k in range(8)]
        for t in range(panel + 1, count):
            leads = spread_columns(tiles[t], panel)
            later = jnp.where((lane >= 8 * panel) & (lane < 8 * panel + 8), 0.0, tiles[t])
            for k in range(8):
                later = later - leads[k] * rows[k]
            tiles[t] = later
        if follows:
            columns = ahead
    inverse = []
    for t in range(size // 8):
        diagonal = lane == sub + 8 * t
        pivots = jnp.sum(jnp.where(diagonal, tiles[t], 0.0), axis=1, keepdims=True)
        unit = jnp.where(diagonal, 1.0, jnp.where(lane < sub + 8 * t, tiles[t], 0.0))
        inverse.append(unit / jnp.sqrt(pivots))
    return jnp.concatenate(inverse, axis=0)


def basis_kernel(
    total_rows, sums_ref, trial_ref, coupled_ref, sigma_ref, projected_ref, basis_ref
):
    size = sums_ref.shape[1]
    scale = 1.0 / total_rows
    overlap = sums_ref[0:size, :] * scale
    projected = sums_ref[size : 2 * size, :] * scale
    projected_ref[...] = projected
    square = sums_ref[2 * size : 3 * size, :] * scale
    row = lax.broadcasted_iota(jnp.int32, (size, size), 0)
    lane = lax.broadcasted_iota(jnp.int32, (size, size), 1)
    middle = jnp.where(row == lane, 2.0, 0.0) - overlap
    folded = jnp.dot(middle, projected, precision=HIGHEST, preferred_element_type=jnp.float32)
    gram = square - lax.dot_general(
        projected, folded, (((0,), (0,)), ((), ())),
        precision=HIGHEST, preferred_element_type=jnp.float32,
    )
    inverse = inverse_factor(gram)
    upper = inverse.T
    pulled = jnp.dot(projected, upper, precision=HIGHEST, preferred_element_type=jnp.float32)
    weights = jnp.concatenate([upper, 0.0 - pulled], axis=0)
    coupled = coupled_ref[...]
    sigma_ref[...] = coupled
    both = jnp.concatenate([coupled, trial_ref[...]], axis=1)
    result = None
    for term in reversed(split_three(weights)):
        product = jnp.dot(both, term, preferred_element_type=jnp.float32)
        result = product if result is None else result + product
    basis_ref[...] = result


def on_device(n_blk, n_col, trial, omega, table, block_type, cycle_offset, source_block):
    row_count, vec_count = trial.shape
    pair_block = table.shape[1]
    blocks = row_count // pair_block
    rows = 2 * vec_count
    near = max(size for size in (4, 2, 1) if n_blk % size == 0)
    group = near * n_col
    far = n_blk // near
    rows = 2 * vec_count
    piece = rows // group
    own_piece = vec_count // group
    vmem = pl.BlockSpec(memory_space=pltpu.VMEM)
    smem = pl.BlockSpec(memory_space=pltpu.SMEM)
    hbm = pl.BlockSpec(memory_space=pltpu.HBM)
    dma = pltpu.SemaphoreType.DMA
    coupled, sums = pl.pallas_call(
        functools.partial(couple_kernel, n_blk, n_col, near),
        out_shape=(
            jax.ShapeDtypeStruct((row_count, vec_count), jnp.bfloat16),
            jax.ShapeDtypeStruct((3 * vec_count, vec_count), jnp.float32),
        ),
        in_specs=[smem, smem, smem, hbm, hbm, hbm],
        out_specs=(vmem, vmem),
        scratch_shapes=[
            pltpu.VMEM(table.shape, jnp.bfloat16),
            pltpu.VMEM(table.shape, jnp.bfloat16),
            pltpu.VMEM((2 * REACH + 1, blocks, pair_block // 2, vec_count), jnp.bfloat16),
            pltpu.VMEM((2 * REACH + 1, blocks, pair_block // 2, vec_count), jnp.bfloat16),
            pltpu.VMEM((blocks, pair_block, vec_count), jnp.bfloat16),
            pltpu.VMEM((vec_count, row_count), jnp.bfloat16),
            pltpu.VMEM((blocks, pair_block), jnp.float32),
            pltpu.VMEM((blocks, pair_block, vec_count), jnp.float32),
            pltpu.VMEM((vec_count, vec_count), jnp.float32),
            pltpu.VMEM((group - 1, own_piece, vec_count), jnp.float32),
            pltpu.VMEM((far, own_piece, vec_count), jnp.float32),
            pltpu.VMEM((vec_count, vec_count), jnp.float32),
            pltpu.VMEM((rows, vec_count), jnp.float32),
            pltpu.VMEM((group - 1, piece, vec_count), jnp.float32),
            pltpu.VMEM((far, piece, vec_count), jnp.float32),
            pltpu.VMEM((rows, vec_count), jnp.float32),
            dma((5,)),
            dma((8, PARTS)),
            dma((8, PARTS)),
            dma((group - 1,)),
            dma((group - 1,)),
            dma((far - 1,)),
            dma((far - 1,)),
            dma((group - 1,)),
            dma((group - 1,)),
            dma((group - 1,)),
            dma((group - 1,)),
            dma((far - 1,)),
            dma((far - 1,)),
            dma((group - 1,)),
            dma((group - 1,)),
        ],
        compiler_params=pltpu.CompilerParams(
            collective_id=0, has_side_effects=True, vmem_limit_bytes=60 << 20
        ),
        name="couple",
    )(
        block_type,
        cycle_offset,
        source_block,
        trial.reshape(blocks, pair_block, vec_count),
        omega.reshape(blocks, pair_block),
        table,
    )
    sigma, projected, basis = pl.pallas_call(
        functools.partial(basis_kernel, row_count * n_blk * n_col),
        out_shape=(
            jax.ShapeDtypeStruct((row_count, vec_count), jnp.bfloat16),
            jax.ShapeDtypeStruct((vec_count, vec_count), jnp.float32),
            jax.ShapeDtypeStruct((row_count, vec_count), jnp.float32),
        ),
        in_specs=[vmem] * 3,
        out_specs=(vmem, vmem, vmem),
        compiler_params=pltpu.CompilerParams(vmem_limit_bytes=60 << 20),
        name="basis",
    )(sums, trial, coupled)
    return (sigma, projected, basis)


def solution(mesh):
    placed = (
        P(("blk", "col"), None),
        P(("blk", "col")),
        P(),
        P(("blk", "col"), None),
        P(("blk", "col"), None),
        P(("blk", "col"), None),
    )
    return jax.shard_map(
        functools.partial(on_device, mesh.shape["blk"], mesh.shape["col"]),
        mesh=mesh,
        in_specs=placed,
        out_specs=(P(("blk", "col"), None), P(), P(("blk", "col"), None)),
        check_vma=False,
    )
```

```python
import functools

import jax
import jax.numpy as jnp
from jax import lax
from jax.experimental import pallas as pl
from jax.experimental.pallas import tpu as pltpu
from jax.sharding import PartitionSpec as P

REACH = 4
MESH = pl.DeviceIdType.MESH
HIGHEST = lax.Precision.HIGHEST
PARTS = 4
HALF = PARTS // 2


def wrap(index, count):
    return lax.rem(index + count, count)


def spread(count, mine, source, target, send, recv, place):
    copies = []
    for step in range(1, count):
        peer = wrap(mine + step, count)
        copy = pltpu.make_async_remote_copy(
            src_ref=source(peer),
            dst_ref=target(step),
            send_sem=send.at[step - 1],
            recv_sem=recv.at[step - 1],
            device_id=place(peer),
            device_id_type=MESH,
        )
        copy.start()
        copies.append(copy)
    return copies


def rows_at(index, size):
    return pl.ds(pl.multiple_of(index * size, 8), size)


def couple_kernel(
    n_blk, n_col, near,
    kinds_ref, cycle_ref, source_ref, trial_hbm, omega_hbm, table_hbm,
    sigma_ref, sums_ref,
    table_ref, turned_ref, first_half, second_half, own_ref, across, omega_ref, acc_ref,
    own_part, own_got, own_ring, own_total,
    part, got, ring, total,
    local_sems, g_send, g_recv,
    o_send, o_recv, oz_send, oz_recv, oa_send, oa_recv,
    r_send, r_recv, z_send, z_recv, a_send, a_recv,
):
    blocks, pair_block, vec_count = trial_hbm.shape
    per_row = kinds_ref.shape[1]
    me_b = lax.axis_index("blk")
    me_c = lax.axis_index("col")

    group = near * n_col
    far = n_blk // near
    low = lax.rem(me_b, near)
    high = me_b // near
    mine = low * n_col + me_c

    def near_id(index):
        return (high * near + index // n_col, lax.rem(index, n_col))

    def far_id(index):
        return (index * near + low, me_c)

    middle = pair_block // 2
    halves = (first_half, second_half)
    keep_half = []
    for which in range(2):
        copy = pltpu.make_async_copy(
            trial_hbm.at[:, pl.ds(which * middle, middle)],
            halves[which].at[REACH],
            local_sems.at[3 + which],
        )
        copy.start()
        keep_half.append(copy)
    keep_own = pltpu.make_async_copy(trial_hbm, own_ref, local_sems.at[0])
    keep_own.start()
    load_omega = pltpu.make_async_copy(omega_hbm, omega_ref, local_sems.at[1])
    load_omega.start()
    load_table = pltpu.make_async_copy(table_hbm, table_ref, local_sems.at[2])
    load_table.start()

    x = lax.rem(low, 2)
    y = low // 2
    ahead = wrap(me_b - REACH + 2 * REACH * y, n_blk)
    behind = wrap(me_b + REACH - 2 * REACH * y, n_blk)
    side_x = me_b + 1 - 2 * x
    side_y = me_b + 2 - 4 * y

    barrier = pltpu.get_barrier_semaphore()
    for step in range(1, far):
        pl.semaphore_signal(
            barrier, inc=1, device_id=far_id(wrap(high + step, far)), device_id_type=MESH
        )
    for step in range(1, group):
        pl.semaphore_signal(
            barrier, inc=1, device_id=near_id(wrap(mine + step, group)), device_id_type=MESH
        )
    pl.semaphore_wait(barrier, group - 1 + far - 1)

    span = blocks // HALF

    def message(number, h, source, slot, target):
        which = h // HALF
        blocks_of = pl.ds((h % HALF) * span, span)
        rows_of = pl.ds(which * middle, middle)
        slabs = halves[which]
        return pltpu.make_async_remote_copy(
            src_ref=trial_hbm.at[blocks_of, rows_of] if source is None else slabs.at[source, blocks_of],
            dst_ref=slabs.at[slot, blocks_of],
            send_sem=g_send.at[number, h],
            recv_sem=g_recv.at[number, h],
            device_id=(target, me_c),
            device_id_type=MESH,
        )

    parts = range(PARTS)
    first_z = [message(0, h, None, 8 - 8 * y, ahead) for h in parts]
    second_z = [message(1, h, None, 8 * y, behind) for h in parts]
    own_x = [message(2, h, None, 3 + 2 * x, side_x) for h in parts]
    own_y = [message(3, h, None, 2 + 4 * y, side_y) for h in parts]
    pass_y = [message(4, h, 5 - 2 * x, 3 - 2 * x + 4 * y, side_y) for h in parts]
    far_x = [message(5, h, 8 - 8 * x, 7 - 6 * x, side_x) for h in parts]
    far_y = [message(6, h, 8 - 8 * y, 6 - 4 * y, side_y) for h in parts]
    pass_x = [message(7, h, 2 + 4 * y, 1 + 4 * y + 2 * x, side_x) for h in parts]

    early = range(HALF)
    late = range(HALF, PARTS)

    def relay_first(h):
        first_z[h].wait_recv()
        far_y[h].start()

        @pl.when(x == y)
        def _():
            far_x[h].start()

    def relay_own(h):
        own_x[h].wait_recv()
        pass_y[h].start()

    def relay_second(h):
        second_z[h].wait_recv()

        @pl.when(x != y)
        def _():
            far_x[h].start()

    def relay_far(h):
        far_y[h].wait_recv()
        pass_x[h].start()

    def arrived(h):
        own_y[h].wait_recv()
        pass_y[h].wait_recv()
        far_x[h].wait_recv()
        pass_x[h].wait_recv()

    for h in early:
        first_z[h].start()
        own_x[h].start()
        own_y[h].start()
    for h in early:
        second_z[h].start()

    load_table.wait()

    def turn(index, carry):
        turned_ref[index] = jnp.roll(table_ref[index], middle, axis=1)
        return carry

    lax.fori_loop(0, table_ref.shape[0], turn, 0, unroll=8)
    keep_own.wait()
    own = own_ref[...].reshape(blocks * pair_block, vec_count)
    across[...] = own.T
    own_part[...] = jnp.dot(across[...], own, preferred_element_type=jnp.float32)
    load_omega.wait()

    for h in early:
        relay_first(h)
        first_z[HALF + h].start()
    for h in late:
        own_x[h].start()
        second_z[h].start()
    for h in early:
        relay_own(h)
    for h in early:
        relay_second(h)
    for h in early:
        relay_far(h)
    for h in late:
        relay_first(h)
    for h in late:
        own_y[h].start()
    for h in late:
        relay_second(h)
    for h in late:
        relay_own(h)
    for h in early:
        arrived(h)
    keep_half[0].wait()
    for h in late:
        relay_far(h)

    def scatter(source, target, send, recv):
        size = target.shape[1]
        return spread(
            group, mine, lambda peer: source.at[rows_at(peer, size)],
            lambda step: target.at[step - 1], send, recv, near_id,
        )

    def across_far(copies, source, target, place, send, recv):
        size = target.shape[1]
        piece = source[rows_at(mine, size), :]
        for step, copy in enumerate(copies):
            copy.wait()
            piece = piece + target[step]
        place[high] = piece
        return spread(
            far, high, lambda peer: place.at[high], lambda step: place.at[high],
            send, recv, far_id,
        )

    def gather(copies, source, target, send, recv):
        for copy in copies:
            copy.wait()
        piece = source[0]
        for index in range(1, far):
            piece = piece + source[index]
        place = rows_at(mine, source.shape[1])
        target[place, :] = piece
        return spread(
            group, mine, lambda peer: target.at[place], lambda step: target.at[place],
            send, recv, near_id,
        )

    pairs = per_row // 2
    chunk = max(size for size in range(1, 9) if pairs % size == 0)
    row_id = lax.broadcasted_iota(jnp.int32, (pair_block, pair_block), 0)
    lane_id = lax.broadcasted_iota(jnp.int32, (pair_block, pair_block), 1)
    left_id = lax.broadcasted_iota(jnp.int32, table_ref.shape[1:], 1) < middle

    def products(r, which, acc):
        left, right = (table_ref, turned_ref) if which == 0 else (turned_ref, table_ref)
        slabs = halves[which]
        for start in range(0, pairs, chunk):
            coeffs = []
            sources = []
            for pair in range(start, start + chunk):
                j = 2 * pair
                coeffs.append(jnp.where(left_id, left[kinds_ref[r, j]], right[kinds_ref[r, j + 1]]))
                sources.append(slabs[cycle_ref[r, j] + REACH, source_ref[r, j]])
                sources.append(slabs[cycle_ref[r, j + 1] + REACH, source_ref[r, j + 1]])
            acc = acc + jnp.dot(
                jnp.concatenate(coeffs, axis=1),
                jnp.concatenate(sources, axis=0),
                preferred_element_type=jnp.float32,
            )
        return acc

    for r in range(blocks):
        energy = jnp.broadcast_to(omega_ref[r : r + 1, :], (pair_block, pair_block))
        column = jnp.sum(jnp.where(row_id == lane_id, energy, 0.0), axis=1, keepdims=True)
        acc_ref[r] = products(r, 0, column * own_ref[r].astype(jnp.float32))

    for h in late:
        arrived(h)
    keep_half[1].wait()
    own_copies = scatter(own_part, own_got, o_send, o_recv)
    sums = None
    for r in range(blocks):
        acc = products(r, 1, acc_ref[r])
        sigma_ref[r * pair_block : (r + 1) * pair_block, :] = acc.astype(jnp.bfloat16)
        if r % 2 == 1:
            place = slice((r - 1) * pair_block, (r + 1) * pair_block)
            sigma = sigma_ref[place, :]
            both = jnp.concatenate([across[:, place], sigma.T], axis=0)
            term = jnp.dot(both, sigma, preferred_element_type=jnp.float32)
            sums = term if sums is None else sums + term
    part[...] = sums

    copies = scatter(part, got, r_send, r_recv)
    own_copies = across_far(own_copies, own_part, own_got, own_ring, oz_send, oz_recv)
    for sent in (first_z, second_z, own_x, own_y, pass_y, far_x, far_y, pass_x):
        for h in parts:
            sent[h].wait_send()
    copies = across_far(copies, part, got, ring, z_send, z_recv)
    own_copies = gather(own_copies, own_ring, own_total, oa_send, oa_recv)
    copies = gather(copies, ring, total, a_send, a_recv)
    for copy in own_copies:
        copy.wait()
    sums_ref[0:vec_count, :] = own_total[...]
    for copy in copies:
        copy.wait()
    sums_ref[vec_count:, :] = total[...]


def split_three(value):
    high = value.astype(jnp.bfloat16)
    rest = value - high.astype(jnp.float32)
    middle = rest.astype(jnp.bfloat16)
    low = (rest - middle.astype(jnp.float32)).astype(jnp.bfloat16)
    return high, middle, low


def inverse_factor(gram):
    size = gram.shape[0]
    count = size // 8
    tiles = [gram[8 * t : 8 * t + 8, :] for t in range(count)]
    lane = lax.broadcasted_iota(jnp.int32, (8, size), 1)
    sub = lax.broadcasted_iota(jnp.int32, (8, size), 0)

    def spread_row(tile, k):
        return jnp.broadcast_to(tile[k : k + 1, :], (8, size))

    def spread_columns(tile, panel):
        return [
            jnp.broadcast_to(tile[:, 8 * panel + k : 8 * panel + k + 1], (8, size))
            for k in range(8)
        ]

    columns = spread_columns(tiles[0], 0)
    for panel in range(count):
        tile = tiles[panel]
        full = tile
        follows = panel + 1 < count
        if follows:
            below = spread_columns(tiles[panel + 1], panel)
            ahead = spread_columns(tiles[panel + 1], panel + 1)
        for k in range(0, 8, 2):
            n = k + 1
            corner = spread_row(columns[k], k)
            side = spread_row(columns[n], k)
            other = spread_row(columns[n], n)
            first = 1.0 / corner
            second = corner * (1.0 / (corner * other - side * side))
            row_k = {m: spread_row(columns[m], k) * first for m in range(n, 8)}
            row_n = {
                m: (spread_row(columns[m], n) - side * row_k[m]) * second for m in range(n + 1, 8)
            }
            lead_k = jnp.where(sub == k, 0.0, columns[k])
            lead_n = jnp.where(sub == n, 0.0, columns[n] - lead_k * row_k[n])
            lead_n = jnp.where(sub == k, row_k[n], lead_n)
            for m in range(n + 1, 8):
                column = jnp.where(sub == k, row_k[m], columns[m] - lead_k * row_k[m])
                columns[m] = jnp.where(sub == n, row_n[m], column - lead_n * row_n[m])
            for lead, reciprocal, at in ((lead_k, first, k), (lead_n, second, n)):
                here = lane == 8 * panel + at
                scaled = jnp.where(here, 1.0, spread_row(tile, at)) * reciprocal
                cleared = jnp.where(here & (sub > at), 0.0, tile)
                tile = cleared - jnp.where(sub > at, lead, 0.0) * scaled
                full = jnp.where(sub == at, scaled, jnp.where(here, 0.0, full) - lead * scaled)
            if follows:
                below[n] = below[n] - below[k] * row_k[n]
                for m in range(n + 1, 8):
                    below[m] = below[m] - below[k] * row_k[m] - below[n] * row_n[m]
                scaled_k = below[k] * first
                scaled_n = below[n] * second
                for m in range(8):
                    ahead[m] = (
                        ahead[m]
                        - below[k] * spread_row(scaled_k, m)
                        - below[n] * spread_row(scaled_n, m)
                    )
        tiles[panel] = tile
        rows = [spread_row(full, k) for k in range(8)]
        for t in range(panel + 1, count):
            leads = spread_columns(tiles[t], panel)
            later = jnp.where((lane >= 8 * panel) & (lane < 8 * panel + 8), 0.0, tiles[t])
            for k in range(8):
                later = later - leads[k] * rows[k]
            tiles[t] = later
        if follows:
            columns = ahead
    inverse = []
    for t in range(size // 8):
        diagonal = lane == sub + 8 * t
        pivots = jnp.sum(jnp.where(diagonal, tiles[t], 0.0), axis=1, keepdims=True)
        unit = jnp.where(diagonal, 1.0, jnp.where(lane < sub + 8 * t, tiles[t], 0.0))
        inverse.append(unit / jnp.sqrt(pivots))
    return jnp.concatenate(inverse, axis=0)


def basis_kernel(
    total_rows, sums_ref, trial_ref, coupled_ref, sigma_ref, projected_ref, basis_ref
):
    size = sums_ref.shape[1]
    scale = 1.0 / total_rows
    overlap = sums_ref[0:size, :] * scale
    projected = sums_ref[size : 2 * size, :] * scale
    projected_ref[...] = projected
    square = sums_ref[2 * size : 3 * size, :] * scale
    row = lax.broadcasted_iota(jnp.int32, (size, size), 0)
    lane = lax.broadcasted_iota(jnp.int32, (size, size), 1)
    middle = jnp.where(row == lane, 2.0, 0.0) - overlap
    folded = jnp.dot(middle, projected, precision=HIGHEST, preferred_element_type=jnp.float32)
    gram = square - lax.dot_general(
        projected, folded, (((0,), (0,)), ((), ())),
        precision=HIGHEST, preferred_element_type=jnp.float32,
    )
    inverse = inverse_factor(gram)
    upper = inverse.T
    pulled = jnp.dot(projected, upper, precision=HIGHEST, preferred_element_type=jnp.float32)
    weights = jnp.concatenate([upper, 0.0 - pulled], axis=0)
    coupled = coupled_ref[...]
    sigma_ref[...] = coupled
    both = jnp.concatenate([coupled, trial_ref[...]], axis=1)
    result = None
    for term in reversed(split_three(weights)):
        product = jnp.dot(both, term, preferred_element_type=jnp.float32)
        result = product if result is None else result + product
    basis_ref[...] = result


def on_device(n_blk, n_col, trial, omega, table, block_type, cycle_offset, source_block):
    row_count, vec_count = trial.shape
    pair_block = table.shape[1]
    blocks = row_count // pair_block
    rows = 2 * vec_count
    near = max(size for size in (4, 2, 1) if n_blk % size == 0)
    group = near * n_col
    far = n_blk // near
    rows = 2 * vec_count
    piece = rows // group
    own_piece = vec_count // group
    vmem = pl.BlockSpec(memory_space=pltpu.VMEM)
    smem = pl.BlockSpec(memory_space=pltpu.SMEM)
    hbm = pl.BlockSpec(memory_space=pltpu.HBM)
    dma = pltpu.SemaphoreType.DMA
    coupled, sums = pl.pallas_call(
        functools.partial(couple_kernel, n_blk, n_col, near),
        out_shape=(
            jax.ShapeDtypeStruct((row_count, vec_count), jnp.bfloat16),
            jax.ShapeDtypeStruct((3 * vec_count, vec_count), jnp.float32),
        ),
        in_specs=[smem, smem, smem, hbm, hbm, hbm],
        out_specs=(vmem, vmem),
        scratch_shapes=[
            pltpu.VMEM(table.shape, jnp.bfloat16),
            pltpu.VMEM(table.shape, jnp.bfloat16),
            pltpu.VMEM((2 * REACH + 1, blocks, pair_block // 2, vec_count), jnp.bfloat16),
            pltpu.VMEM((2 * REACH + 1, blocks, pair_block // 2, vec_count), jnp.bfloat16),
            pltpu.VMEM((blocks, pair_block, vec_count), jnp.bfloat16),
            pltpu.VMEM((vec_count, row_count), jnp.bfloat16),
            pltpu.VMEM((blocks, pair_block), jnp.float32),
            pltpu.VMEM((blocks, pair_block, vec_count), jnp.float32),
            pltpu.VMEM((vec_count, vec_count), jnp.float32),
            pltpu.VMEM((group - 1, own_piece, vec_count), jnp.float32),
            pltpu.VMEM((far, own_piece, vec_count), jnp.float32),
            pltpu.VMEM((vec_count, vec_count), jnp.float32),
            pltpu.VMEM((rows, vec_count), jnp.float32),
            pltpu.VMEM((group - 1, piece, vec_count), jnp.float32),
            pltpu.VMEM((far, piece, vec_count), jnp.float32),
            pltpu.VMEM((rows, vec_count), jnp.float32),
            dma((5,)),
            dma((8, PARTS)),
            dma((8, PARTS)),
            dma((group - 1,)),
            dma((group - 1,)),
            dma((far - 1,)),
            dma((far - 1,)),
            dma((group - 1,)),
            dma((group - 1,)),
            dma((group - 1,)),
            dma((group - 1,)),
            dma((far - 1,)),
            dma((far - 1,)),
            dma((group - 1,)),
            dma((group - 1,)),
        ],
        compiler_params=pltpu.CompilerParams(
            collective_id=0, has_side_effects=True, vmem_limit_bytes=24 << 20
        ),
        name="couple",
    )(
        *(
            pltpu.with_memory_space_constraint(operand, pltpu.HBM)
            for operand in (
                block_type,
                cycle_offset,
                source_block,
                trial.reshape(blocks, pair_block, vec_count),
                omega.reshape(blocks, pair_block),
                table,
            )
        )
    )
    sigma, projected, basis = pl.pallas_call(
        functools.partial(basis_kernel, row_count * n_blk * n_col),
        out_shape=(
            jax.ShapeDtypeStruct((row_count, vec_count), jnp.bfloat16),
            jax.ShapeDtypeStruct((vec_count, vec_count), jnp.float32),
            jax.ShapeDtypeStruct((row_count, vec_count), jnp.float32),
        ),
        in_specs=[vmem] * 3,
        out_specs=(vmem, vmem, vmem),
        compiler_params=pltpu.CompilerParams(vmem_limit_bytes=24 << 20),
        name="basis",
    )(sums, trial, coupled)
    return (sigma, projected, basis)


def solution(mesh):
    placed = (
        P(("blk", "col"), None),
        P(("blk", "col")),
        P(),
        P(("blk", "col"), None),
        P(("blk", "col"), None),
        P(("blk", "col"), None),
    )
    return jax.shard_map(
        functools.partial(on_device, mesh.shape["blk"], mesh.shape["col"]),
        mesh=mesh,
        in_specs=placed,
        out_specs=(P(("blk", "col"), None), P(), P(("blk", "col"), None)),
        check_vma=False,
    )
```

```python
import functools

import jax
import jax.numpy as jnp
from jax import lax
from jax.experimental import pallas as pl
from jax.experimental.pallas import tpu as pltpu
from jax.sharding import PartitionSpec as P

REACH = 4
MESH = pl.DeviceIdType.MESH
HIGHEST = lax.Precision.HIGHEST
PARTS = 4
HALF = PARTS // 2


def wrap(index, count):
    return lax.rem(index + count, count)


def spread(count, mine, source, target, send, recv, place):
    copies = []
    for step in range(1, count):
        peer = wrap(mine + step, count)
        copy = pltpu.make_async_remote_copy(
            src_ref=source(peer),
            dst_ref=target(step),
            send_sem=send.at[step - 1],
            recv_sem=recv.at[step - 1],
            device_id=place(peer),
            device_id_type=MESH,
        )
        copy.start()
        copies.append(copy)
    return copies


def rows_at(index, size):
    return pl.ds(pl.multiple_of(index * size, 8), size)


def couple_kernel(
    n_blk, n_col, near,
    kinds_hbm, cycle_hbm, source_hbm, trial_hbm, omega_hbm, table_hbm,
    sigma_ref, sums_ref,
    kinds_ref, cycle_ref, source_ref, table_ref, turned_ref, first_half, second_half, own_ref, across, omega_ref, acc_ref,
    own_part, own_got, own_ring, own_total,
    part, got, ring, total,
    local_sems, g_send, g_recv,
    o_send, o_recv, oz_send, oz_recv, oa_send, oa_recv,
    r_send, r_recv, z_send, z_recv, a_send, a_recv,
):
    blocks, pair_block, vec_count = trial_hbm.shape
    per_row = kinds_hbm.shape[1]
    me_b = lax.axis_index("blk")
    me_c = lax.axis_index("col")

    group = near * n_col
    far = n_blk // near
    low = lax.rem(me_b, near)
    high = me_b // near
    mine = low * n_col + me_c

    def near_id(index):
        return (high * near + index // n_col, lax.rem(index, n_col))

    def far_id(index):
        return (index * near + low, me_c)

    middle = pair_block // 2
    halves = (first_half, second_half)
    keep_half = []
    for which in range(2):
        copy = pltpu.make_async_copy(
            trial_hbm.at[:, pl.ds(which * middle, middle)],
            halves[which].at[REACH],
            local_sems.at[3 + which],
        )
        copy.start()
        keep_half.append(copy)
    keep_own = pltpu.make_async_copy(trial_hbm, own_ref, local_sems.at[0])
    keep_own.start()
    load_omega = pltpu.make_async_copy(omega_hbm, omega_ref, local_sems.at[1])
    load_omega.start()
    load_table = pltpu.make_async_copy(table_hbm, table_ref, local_sems.at[2])
    load_table.start()
    load_lists = []
    for at, (source, target) in enumerate(
        ((kinds_hbm, kinds_ref), (cycle_hbm, cycle_ref), (source_hbm, source_ref))
    ):
        copy = pltpu.make_async_copy(source, target, local_sems.at[5 + at])
        copy.start()
        load_lists.append(copy)

    x = lax.rem(low, 2)
    y = low // 2
    ahead = wrap(me_b - REACH + 2 * REACH * y, n_blk)
    behind = wrap(me_b + REACH - 2 * REACH * y, n_blk)
    side_x = me_b + 1 - 2 * x
    side_y = me_b + 2 - 4 * y

    barrier = pltpu.get_barrier_semaphore()
    for step in range(1, far):
        pl.semaphore_signal(
            barrier, inc=1, device_id=far_id(wrap(high + step, far)), device_id_type=MESH
        )
    for step in range(1, group):
        pl.semaphore_signal(
            barrier, inc=1, device_id=near_id(wrap(mine + step, group)), device_id_type=MESH
        )
    pl.semaphore_wait(barrier, group - 1 + far - 1)

    span = blocks // HALF

    def message(number, h, source, slot, target):
        which = h // HALF
        blocks_of = pl.ds((h % HALF) * span, span)
        rows_of = pl.ds(which * middle, middle)
        slabs = halves[which]
        return pltpu.make_async_remote_copy(
            src_ref=trial_hbm.at[blocks_of, rows_of] if source is None else slabs.at[source, blocks_of],
            dst_ref=slabs.at[slot, blocks_of],
            send_sem=g_send.at[number, h],
            recv_sem=g_recv.at[number, h],
            device_id=(target, me_c),
            device_id_type=MESH,
        )

    parts = range(PARTS)
    first_z = [message(0, h, None, 8 - 8 * y, ahead) for h in parts]
    second_z = [message(1, h, None, 8 * y, behind) for h in parts]
    own_x = [message(2, h, None, 3 + 2 * x, side_x) for h in parts]
    own_y = [message(3, h, None, 2 + 4 * y, side_y) for h in parts]
    pass_y = [message(4, h, 5 - 2 * x, 3 - 2 * x + 4 * y, side_y) for h in parts]
    far_x = [message(5, h, 8 - 8 * x, 7 - 6 * x, side_x) for h in parts]
    far_y = [message(6, h, 8 - 8 * y, 6 - 4 * y, side_y) for h in parts]
    pass_x = [message(7, h, 2 + 4 * y, 1 + 4 * y + 2 * x, side_x) for h in parts]

    early = range(HALF)
    late = range(HALF, PARTS)

    def relay_first(h):
        first_z[h].wait_recv()
        far_y[h].start()

        @pl.when(x == y)
        def _():
            far_x[h].start()

    def relay_own(h):
        own_x[h].wait_recv()
        pass_y[h].start()

    def relay_second(h):
        second_z[h].wait_recv()

        @pl.when(x != y)
        def _():
            far_x[h].start()

    def relay_far(h):
        far_y[h].wait_recv()
        pass_x[h].start()

    def arrived(h):
        own_y[h].wait_recv()
        pass_y[h].wait_recv()
        far_x[h].wait_recv()
        pass_x[h].wait_recv()

    for h in early:
        first_z[h].start()
        own_x[h].start()
        own_y[h].start()
    for h in early:
        second_z[h].start()

    load_table.wait()

    def turn(index, carry):
        turned_ref[index] = jnp.roll(table_ref[index], middle, axis=1)
        return carry

    lax.fori_loop(0, table_ref.shape[0], turn, 0, unroll=8)
    keep_own.wait()
    own = own_ref[...].reshape(blocks * pair_block, vec_count)
    across[...] = own.T
    own_part[...] = jnp.dot(across[...], own, preferred_element_type=jnp.float32)
    load_omega.wait()
    for copy in load_lists:
        copy.wait()

    for h in early:
        relay_first(h)
        first_z[HALF + h].start()
    for h in late:
        own_x[h].start()
        second_z[h].start()
    for h in early:
        relay_own(h)
    for h in early:
        relay_second(h)
    for h in early:
        relay_far(h)
    for h in late:
        relay_first(h)
    for h in late:
        own_y[h].start()
    for h in late:
        relay_second(h)
    for h in late:
        relay_own(h)
    for h in early:
        arrived(h)
    keep_half[0].wait()
    for h in late:
        relay_far(h)

    def scatter(source, target, send, recv):
        size = target.shape[1]
        return spread(
            group, mine, lambda peer: source.at[rows_at(peer, size)],
            lambda step: target.at[step - 1], send, recv, near_id,
        )

    def across_far(copies, source, target, place, send, recv):
        size = target.shape[1]
        piece = source[rows_at(mine, size), :]
        for step, copy in enumerate(copies):
            copy.wait()
            piece = piece + target[step]
        place[high] = piece
        return spread(
            far, high, lambda peer: place.at[high], lambda step: place.at[high],
            send, recv, far_id,
        )

    def gather(copies, source, target, send, recv):
        for copy in copies:
            copy.wait()
        piece = source[0]
        for index in range(1, far):
            piece = piece + source[index]
        place = rows_at(mine, source.shape[1])
        target[place, :] = piece
        return spread(
            group, mine, lambda peer: target.at[place], lambda step: target.at[place],
            send, recv, near_id,
        )

    pairs = per_row // 2
    chunk = max(size for size in range(1, 9) if pairs % size == 0)
    row_id = lax.broadcasted_iota(jnp.int32, (pair_block, pair_block), 0)
    lane_id = lax.broadcasted_iota(jnp.int32, (pair_block, pair_block), 1)
    left_id = lax.broadcasted_iota(jnp.int32, table_ref.shape[1:], 1) < middle

    def products(r, which, acc):
        left, right = (table_ref, turned_ref) if which == 0 else (turned_ref, table_ref)
        slabs = halves[which]
        for start in range(0, pairs, chunk):
            coeffs = []
            sources = []
            for pair in range(start, start + chunk):
                j = 2 * pair
                coeffs.append(jnp.where(left_id, left[kinds_ref[r, j]], right[kinds_ref[r, j + 1]]))
                sources.append(slabs[cycle_ref[r, j] + REACH, source_ref[r, j]])
                sources.append(slabs[cycle_ref[r, j + 1] + REACH, source_ref[r, j + 1]])
            acc = acc + jnp.dot(
                jnp.concatenate(coeffs, axis=1),
                jnp.concatenate(sources, axis=0),
                preferred_element_type=jnp.float32,
            )
        return acc

    for r in range(blocks):
        energy = jnp.broadcast_to(omega_ref[r : r + 1, :], (pair_block, pair_block))
        column = jnp.sum(jnp.where(row_id == lane_id, energy, 0.0), axis=1, keepdims=True)
        acc_ref[r] = products(r, 0, column * own_ref[r].astype(jnp.float32))

    for h in late:
        arrived(h)
    keep_half[1].wait()
    own_copies = scatter(own_part, own_got, o_send, o_recv)
    sums = None
    for r in range(blocks):
        acc = products(r, 1, acc_ref[r])
        sigma_ref[r * pair_block : (r + 1) * pair_block, :] = acc.astype(jnp.bfloat16)
        if r % 2 == 1:
            place = slice((r - 1) * pair_block, (r + 1) * pair_block)
            sigma = sigma_ref[place, :]
            both = jnp.concatenate([across[:, place], sigma.T], axis=0)
            term = jnp.dot(both, sigma, preferred_element_type=jnp.float32)
            sums = term if sums is None else sums + term
    part[...] = sums

    copies = scatter(part, got, r_send, r_recv)
    own_copies = across_far(own_copies, own_part, own_got, own_ring, oz_send, oz_recv)
    for sent in (first_z, second_z, own_x, own_y, pass_y, far_x, far_y, pass_x):
        for h in parts:
            sent[h].wait_send()
    copies = across_far(copies, part, got, ring, z_send, z_recv)
    own_copies = gather(own_copies, own_ring, own_total, oa_send, oa_recv)
    copies = gather(copies, ring, total, a_send, a_recv)
    for copy in own_copies:
        copy.wait()
    sums_ref[0:vec_count, :] = own_total[...]
    for copy in copies:
        copy.wait()
    sums_ref[vec_count:, :] = total[...]


def split_three(value):
    high = value.astype(jnp.bfloat16)
    rest = value - high.astype(jnp.float32)
    middle = rest.astype(jnp.bfloat16)
    low = (rest - middle.astype(jnp.float32)).astype(jnp.bfloat16)
    return high, middle, low


def inverse_factor(gram):
    size = gram.shape[0]
    count = size // 8
    tiles = [gram[8 * t : 8 * t + 8, :] for t in range(count)]
    lane = lax.broadcasted_iota(jnp.int32, (8, size), 1)
    sub = lax.broadcasted_iota(jnp.int32, (8, size), 0)

    def spread_row(tile, k):
        return jnp.broadcast_to(tile[k : k + 1, :], (8, size))

    def spread_columns(tile, panel):
        return [
            jnp.broadcast_to(tile[:, 8 * panel + k : 8 * panel + k + 1], (8, size))
            for k in range(8)
        ]

    columns = spread_columns(tiles[0], 0)
    for panel in range(count):
        tile = tiles[panel]
        full = tile
        follows = panel + 1 < count
        if follows:
            below = spread_columns(tiles[panel + 1], panel)
            ahead = spread_columns(tiles[panel + 1], panel + 1)
        for k in range(0, 8, 2):
            n = k + 1
            corner = spread_row(columns[k], k)
            side = spread_row(columns[n], k)
            other = spread_row(columns[n], n)
            first = 1.0 / corner
            second = corner * (1.0 / (corner * other - side * side))
            row_k = {m: spread_row(columns[m], k) * first for m in range(n, 8)}
            row_n = {
                m: (spread_row(columns[m], n) - side * row_k[m]) * second for m in range(n + 1, 8)
            }
            lead_k = jnp.where(sub == k, 0.0, columns[k])
            lead_n = jnp.where(sub == n, 0.0, columns[n] - lead_k * row_k[n])
            lead_n = jnp.where(sub == k, row_k[n], lead_n)
            for m in range(n + 1, 8):
                column = jnp.where(sub == k, row_k[m], columns[m] - lead_k * row_k[m])
                columns[m] = jnp.where(sub == n, row_n[m], column - lead_n * row_n[m])
            for lead, reciprocal, at in ((lead_k, first, k), (lead_n, second, n)):
                here = lane == 8 * panel + at
                scaled = jnp.where(here, 1.0, spread_row(tile, at)) * reciprocal
                cleared = jnp.where(here & (sub > at), 0.0, tile)
                tile = cleared - jnp.where(sub > at, lead, 0.0) * scaled
                full = jnp.where(sub == at, scaled, jnp.where(here, 0.0, full) - lead * scaled)
            if follows:
                below[n] = below[n] - below[k] * row_k[n]
                for m in range(n + 1, 8):
                    below[m] = below[m] - below[k] * row_k[m] - below[n] * row_n[m]
                scaled_k = below[k] * first
                scaled_n = below[n] * second
                for m in range(8):
                    ahead[m] = (
                        ahead[m]
                        - below[k] * spread_row(scaled_k, m)
                        - below[n] * spread_row(scaled_n, m)
                    )
        tiles[panel] = tile
        rows = [spread_row(full, k) for k in range(8)]
        for t in range(panel + 1, count):
            leads = spread_columns(tiles[t], panel)
            later = jnp.where((lane >= 8 * panel) & (lane < 8 * panel + 8), 0.0, tiles[t])
            for k in range(8):
                later = later - leads[k] * rows[k]
            tiles[t] = later
        if follows:
            columns = ahead
    inverse = []
    for t in range(size // 8):
        diagonal = lane == sub + 8 * t
        pivots = jnp.sum(jnp.where(diagonal, tiles[t], 0.0), axis=1, keepdims=True)
        unit = jnp.where(diagonal, 1.0, jnp.where(lane < sub + 8 * t, tiles[t], 0.0))
        inverse.append(unit / jnp.sqrt(pivots))
    return jnp.concatenate(inverse, axis=0)


def basis_kernel(
    total_rows, sums_ref, trial_ref, coupled_ref, sigma_ref, projected_ref, basis_ref
):
    size = sums_ref.shape[1]
    scale = 1.0 / total_rows
    overlap = sums_ref[0:size, :] * scale
    projected = sums_ref[size : 2 * size, :] * scale
    projected_ref[...] = projected
    square = sums_ref[2 * size : 3 * size, :] * scale
    row = lax.broadcasted_iota(jnp.int32, (size, size), 0)
    lane = lax.broadcasted_iota(jnp.int32, (size, size), 1)
    middle = jnp.where(row == lane, 2.0, 0.0) - overlap
    folded = jnp.dot(middle, projected, precision=HIGHEST, preferred_element_type=jnp.float32)
    gram = square - lax.dot_general(
        projected, folded, (((0,), (0,)), ((), ())),
        precision=HIGHEST, preferred_element_type=jnp.float32,
    )
    inverse = inverse_factor(gram)
    upper = inverse.T
    pulled = jnp.dot(projected, upper, precision=HIGHEST, preferred_element_type=jnp.float32)
    weights = jnp.concatenate([upper, 0.0 - pulled], axis=0)
    coupled = coupled_ref[...]
    sigma_ref[...] = coupled
    both = jnp.concatenate([coupled, trial_ref[...]], axis=1)
    result = None
    for term in reversed(split_three(weights)):
        product = jnp.dot(both, term, preferred_element_type=jnp.float32)
        result = product if result is None else result + product
    basis_ref[...] = result


def on_device(n_blk, n_col, trial, omega, table, block_type, cycle_offset, source_block):
    row_count, vec_count = trial.shape
    pair_block = table.shape[1]
    blocks = row_count // pair_block
    rows = 2 * vec_count
    near = max(size for size in (4, 2, 1) if n_blk % size == 0)
    group = near * n_col
    far = n_blk // near
    rows = 2 * vec_count
    piece = rows // group
    own_piece = vec_count // group
    vmem = pl.BlockSpec(memory_space=pltpu.VMEM)
    hbm = pl.BlockSpec(memory_space=pltpu.HBM)
    dma = pltpu.SemaphoreType.DMA
    coupled, sums = pl.pallas_call(
        functools.partial(couple_kernel, n_blk, n_col, near),
        out_shape=(
            jax.ShapeDtypeStruct((row_count, vec_count), jnp.bfloat16),
            jax.ShapeDtypeStruct((3 * vec_count, vec_count), jnp.float32),
        ),
        in_specs=[hbm] * 6,
        out_specs=(vmem, vmem),
        scratch_shapes=[
            pltpu.SMEM(block_type.shape, jnp.int32),
            pltpu.SMEM(block_type.shape, jnp.int32),
            pltpu.SMEM(block_type.shape, jnp.int32),
            pltpu.VMEM(table.shape, jnp.bfloat16),
            pltpu.VMEM(table.shape, jnp.bfloat16),
            pltpu.VMEM((2 * REACH + 1, blocks, pair_block // 2, vec_count), jnp.bfloat16),
            pltpu.VMEM((2 * REACH + 1, blocks, pair_block // 2, vec_count), jnp.bfloat16),
            pltpu.VMEM((blocks, pair_block, vec_count), jnp.bfloat16),
            pltpu.VMEM((vec_count, row_count), jnp.bfloat16),
            pltpu.VMEM((blocks, pair_block), jnp.float32),
            pltpu.VMEM((blocks, pair_block, vec_count), jnp.float32),
            pltpu.VMEM((vec_count, vec_count), jnp.float32),
            pltpu.VMEM((group - 1, own_piece, vec_count), jnp.float32),
            pltpu.VMEM((far, own_piece, vec_count), jnp.float32),
            pltpu.VMEM((vec_count, vec_count), jnp.float32),
            pltpu.VMEM((rows, vec_count), jnp.float32),
            pltpu.VMEM((group - 1, piece, vec_count), jnp.float32),
            pltpu.VMEM((far, piece, vec_count), jnp.float32),
            pltpu.VMEM((rows, vec_count), jnp.float32),
            dma((8,)),
            dma((8, PARTS)),
            dma((8, PARTS)),
            dma((group - 1,)),
            dma((group - 1,)),
            dma((far - 1,)),
            dma((far - 1,)),
            dma((group - 1,)),
            dma((group - 1,)),
            dma((group - 1,)),
            dma((group - 1,)),
            dma((far - 1,)),
            dma((far - 1,)),
            dma((group - 1,)),
            dma((group - 1,)),
        ],
        compiler_params=pltpu.CompilerParams(
            collective_id=0, has_side_effects=True, vmem_limit_bytes=24 << 20
        ),
        name="couple",
    )(
        *(
            pltpu.with_memory_space_constraint(operand, pltpu.HBM)
            for operand in (
                block_type,
                cycle_offset,
                source_block,
                trial.reshape(blocks, pair_block, vec_count),
                omega.reshape(blocks, pair_block),
                table,
            )
        )
    )
    sigma, projected, basis = pl.pallas_call(
        functools.partial(basis_kernel, row_count * n_blk * n_col),
        out_shape=(
            jax.ShapeDtypeStruct((row_count, vec_count), jnp.bfloat16),
            jax.ShapeDtypeStruct((vec_count, vec_count), jnp.float32),
            jax.ShapeDtypeStruct((row_count, vec_count), jnp.float32),
        ),
        in_specs=[vmem] * 3,
        out_specs=(vmem, vmem, vmem),
        compiler_params=pltpu.CompilerParams(vmem_limit_bytes=24 << 20),
        name="basis",
    )(sums, trial, coupled)
    return (sigma, projected, basis)


def solution(mesh):
    placed = (
        P(("blk", "col"), None),
        P(("blk", "col")),
        P(),
        P(("blk", "col"), None),
        P(("blk", "col"), None),
        P(("blk", "col"), None),
    )
    return jax.shard_map(
        functools.partial(on_device, mesh.shape["blk"], mesh.shape["col"]),
        mesh=mesh,
        in_specs=placed,
        out_specs=(P(("blk", "col"), None), P(), P(("blk", "col"), None)),
        check_vma=False,
    )
```

```python
import functools

import jax
import jax.numpy as jnp
from jax import lax
from jax.experimental import pallas as pl
from jax.experimental.pallas import tpu as pltpu
from jax.sharding import PartitionSpec as P

REACH = 4
MESH = pl.DeviceIdType.MESH
HIGHEST = lax.Precision.HIGHEST
PARTS = 4
HALF = PARTS // 2


def wrap(index, count):
    return lax.rem(index + count, count)


def spread(count, mine, source, target, send, recv, place):
    copies = []
    for step in range(1, count):
        peer = wrap(mine + step, count)
        copy = pltpu.make_async_remote_copy(
            src_ref=source(peer),
            dst_ref=target(step),
            send_sem=send.at[step - 1],
            recv_sem=recv.at[step - 1],
            device_id=place(peer),
            device_id_type=MESH,
        )
        copy.start()
        copies.append(copy)
    return copies


def rows_at(index, size):
    return pl.ds(pl.multiple_of(index * size, 8), size)


def couple_kernel(
    n_blk, n_col, near,
    kinds_hbm, cycle_hbm, source_hbm, trial_hbm, omega_hbm, table_hbm,
    sigma_ref, sums_ref,
    kinds_ref, cycle_ref, source_ref, table_ref, turned_ref, first_half, second_half, own_ref, across, omega_ref, acc_ref,
    own_part, own_got, own_ring, own_total,
    part, got, ring, total,
    local_sems, g_send, g_recv,
    o_send, o_recv, oz_send, oz_recv, oa_send, oa_recv,
    r_send, r_recv, z_send, z_recv, a_send, a_recv,
):
    blocks, pair_block, vec_count = trial_hbm.shape
    per_row = kinds_hbm.shape[1]
    me_b = lax.axis_index("blk")
    me_c = lax.axis_index("col")

    group = near * n_col
    far = n_blk // near
    low = lax.rem(me_b, near)
    high = me_b // near
    mine = low * n_col + me_c

    def near_id(index):
        return (high * near + index // n_col, lax.rem(index, n_col))

    def far_id(index):
        return (index * near + low, me_c)

    barrier = pltpu.get_barrier_semaphore()
    for step in range(1, far):
        pl.semaphore_signal(
            barrier, inc=1, device_id=far_id(wrap(high + step, far)), device_id_type=MESH
        )
    for step in range(1, group):
        pl.semaphore_signal(
            barrier, inc=1, device_id=near_id(wrap(mine + step, group)), device_id_type=MESH
        )
    middle = pair_block // 2
    halves = (first_half, second_half)
    keep_half = []
    for which in range(2):
        copy = pltpu.make_async_copy(
            trial_hbm.at[:, pl.ds(which * middle, middle)],
            halves[which].at[REACH],
            local_sems.at[3 + which],
        )
        copy.start()
        keep_half.append(copy)
    keep_own = pltpu.make_async_copy(trial_hbm, own_ref, local_sems.at[0])
    keep_own.start()
    load_omega = pltpu.make_async_copy(omega_hbm, omega_ref, local_sems.at[1])
    load_omega.start()
    load_table = pltpu.make_async_copy(table_hbm, table_ref, local_sems.at[2])
    load_table.start()
    load_lists = []
    for at, (source, target) in enumerate(
        ((kinds_hbm, kinds_ref), (cycle_hbm, cycle_ref), (source_hbm, source_ref))
    ):
        copy = pltpu.make_async_copy(source, target, local_sems.at[5 + at])
        copy.start()
        load_lists.append(copy)

    x = lax.rem(low, 2)
    y = low // 2
    ahead = wrap(me_b - REACH + 2 * REACH * y, n_blk)
    behind = wrap(me_b + REACH - 2 * REACH * y, n_blk)
    side_x = me_b + 1 - 2 * x
    side_y = me_b + 2 - 4 * y

    pl.semaphore_wait(barrier, group - 1 + far - 1)

    span = blocks // HALF

    def message(number, h, source, slot, target):
        which = h // HALF
        blocks_of = pl.ds((h % HALF) * span, span)
        rows_of = pl.ds(which * middle, middle)
        slabs = halves[which]
        return pltpu.make_async_remote_copy(
            src_ref=trial_hbm.at[blocks_of, rows_of] if source is None else slabs.at[source, blocks_of],
            dst_ref=slabs.at[slot, blocks_of],
            send_sem=g_send.at[number, h],
            recv_sem=g_recv.at[number, h],
            device_id=(target, me_c),
            device_id_type=MESH,
        )

    parts = range(PARTS)
    first_z = [message(0, h, None, 8 - 8 * y, ahead) for h in parts]
    second_z = [message(1, h, None, 8 * y, behind) for h in parts]
    own_x = [message(2, h, None, 3 + 2 * x, side_x) for h in parts]
    own_y = [message(3, h, None, 2 + 4 * y, side_y) for h in parts]
    pass_y = [message(4, h, 5 - 2 * x, 3 - 2 * x + 4 * y, side_y) for h in parts]
    far_x = [message(5, h, 8 - 8 * x, 7 - 6 * x, side_x) for h in parts]
    far_y = [message(6, h, 8 - 8 * y, 6 - 4 * y, side_y) for h in parts]
    pass_x = [message(7, h, 2 + 4 * y, 1 + 4 * y + 2 * x, side_x) for h in parts]

    early = range(HALF)
    late = range(HALF, PARTS)

    def relay_first(h):
        first_z[h].wait_recv()
        far_y[h].start()

        @pl.when(x == y)
        def _():
            far_x[h].start()

    def relay_own(h):
        own_x[h].wait_recv()
        pass_y[h].start()

    def relay_second(h):
        second_z[h].wait_recv()

        @pl.when(x != y)
        def _():
            far_x[h].start()

    def relay_far(h):
        far_y[h].wait_recv()
        pass_x[h].start()

    def arrived(h):
        own_y[h].wait_recv()
        pass_y[h].wait_recv()
        far_x[h].wait_recv()
        pass_x[h].wait_recv()

    for h in early:
        first_z[h].start()
        own_x[h].start()
        own_y[h].start()
    for h in early:
        second_z[h].start()

    load_table.wait()

    def turn(index, carry):
        turned_ref[index] = jnp.roll(table_ref[index], middle, axis=1)
        return carry

    lax.fori_loop(0, table_ref.shape[0], turn, 0, unroll=8)
    load_omega.wait()
    for copy in load_lists:
        copy.wait()

    for h in early:
        relay_first(h)
        first_z[HALF + h].start()
    for h in late:
        own_x[h].start()
        second_z[h].start()
    for h in early:
        relay_own(h)
    for h in early:
        relay_second(h)
    for h in early:
        relay_far(h)
    keep_own.wait()
    own = own_ref[...].reshape(blocks * pair_block, vec_count)
    across[...] = own.T
    own_part[...] = jnp.dot(across[...], own, preferred_element_type=jnp.float32)
    for h in late:
        relay_first(h)
    for h in late:
        own_y[h].start()
    for h in late:
        relay_second(h)
    for h in late:
        relay_own(h)
    for h in early:
        arrived(h)
    keep_half[0].wait()
    for h in late:
        relay_far(h)

    def scatter(source, target, send, recv):
        size = target.shape[1]
        return spread(
            group, mine, lambda peer: source.at[rows_at(peer, size)],
            lambda step: target.at[step - 1], send, recv, near_id,
        )

    def across_far(copies, source, target, place, send, recv):
        size = target.shape[1]
        piece = source[rows_at(mine, size), :]
        for step, copy in enumerate(copies):
            copy.wait()
            piece = piece + target[step]
        place[high] = piece
        return spread(
            far, high, lambda peer: place.at[high], lambda step: place.at[high],
            send, recv, far_id,
        )

    def gather(copies, source, target, send, recv):
        for copy in copies:
            copy.wait()
        piece = source[0]
        for index in range(1, far):
            piece = piece + source[index]
        place = rows_at(mine, source.shape[1])
        target[place, :] = piece
        return spread(
            group, mine, lambda peer: target.at[place], lambda step: target.at[place],
            send, recv, near_id,
        )

    pairs = per_row // 2
    chunk = max(size for size in range(1, 9) if pairs % size == 0)
    row_id = lax.broadcasted_iota(jnp.int32, (pair_block, pair_block), 0)
    lane_id = lax.broadcasted_iota(jnp.int32, (pair_block, pair_block), 1)
    left_id = lax.broadcasted_iota(jnp.int32, table_ref.shape[1:], 1) < middle

    def products(r, which, acc):
        left, right = (table_ref, turned_ref) if which == 0 else (turned_ref, table_ref)
        slabs = halves[which]
        for start in range(0, pairs, chunk):
            coeffs = []
            sources = []
            for pair in range(start, start + chunk):
                j = 2 * pair
                coeffs.append(jnp.where(left_id, left[kinds_ref[r, j]], right[kinds_ref[r, j + 1]]))
                sources.append(slabs[cycle_ref[r, j] + REACH, source_ref[r, j]])
                sources.append(slabs[cycle_ref[r, j + 1] + REACH, source_ref[r, j + 1]])
            acc = acc + jnp.dot(
                jnp.concatenate(coeffs, axis=1),
                jnp.concatenate(sources, axis=0),
                preferred_element_type=jnp.float32,
            )
        return acc

    for r in range(blocks):
        energy = jnp.broadcast_to(omega_ref[r : r + 1, :], (pair_block, pair_block))
        column = jnp.sum(jnp.where(row_id == lane_id, energy, 0.0), axis=1, keepdims=True)
        acc_ref[r] = products(r, 0, column * own_ref[r].astype(jnp.float32))

    for h in late:
        arrived(h)
    keep_half[1].wait()
    own_copies = scatter(own_part, own_got, o_send, o_recv)
    sums = None
    for r in range(blocks):
        acc = products(r, 1, acc_ref[r])
        sigma_ref[r * pair_block : (r + 1) * pair_block, :] = acc.astype(jnp.bfloat16)
        if r % 2 == 0:
            turned = acc.astype(jnp.bfloat16).T
        else:
            place = slice((r - 1) * pair_block, (r + 1) * pair_block)
            sigma = sigma_ref[place, :]
            turned = jnp.concatenate([turned, acc.astype(jnp.bfloat16).T], axis=1)
            both = jnp.concatenate([across[:, place], turned], axis=0)
            term = jnp.dot(both, sigma, preferred_element_type=jnp.float32)
            sums = term if sums is None else sums + term
    part[...] = sums

    copies = scatter(part, got, r_send, r_recv)
    own_copies = across_far(own_copies, own_part, own_got, own_ring, oz_send, oz_recv)
    copies = across_far(copies, part, got, ring, z_send, z_recv)
    own_copies = gather(own_copies, own_ring, own_total, oa_send, oa_recv)
    copies = gather(copies, ring, total, a_send, a_recv)
    for sent in (first_z, second_z, own_x, own_y, pass_y, far_x, far_y, pass_x):
        for h in parts:
            sent[h].wait_send()
    for copy in own_copies:
        copy.wait()
    sums_ref[0:vec_count, :] = own_total[...]
    for copy in copies:
        copy.wait()
    sums_ref[vec_count:, :] = total[...]


def split_three(value):
    high = value.astype(jnp.bfloat16)
    rest = value - high.astype(jnp.float32)
    middle = rest.astype(jnp.bfloat16)
    low = (rest - middle.astype(jnp.float32)).astype(jnp.bfloat16)
    return high, middle, low


def inverse_factor(gram):
    size = gram.shape[0]
    count = size // 8
    tiles = [gram[8 * t : 8 * t + 8, :] for t in range(count)]
    lane = lax.broadcasted_iota(jnp.int32, (8, size), 1)
    sub = lax.broadcasted_iota(jnp.int32, (8, size), 0)

    def spread_row(tile, k):
        return jnp.broadcast_to(tile[k : k + 1, :], (8, size))

    def spread_columns(tile, panel):
        return [
            jnp.broadcast_to(tile[:, 8 * panel + k : 8 * panel + k + 1], (8, size))
            for k in range(8)
        ]

    columns = spread_columns(tiles[0], 0)
    for panel in range(count):
        tile = tiles[panel]
        full = tile
        follows = panel + 1 < count
        if follows:
            below = spread_columns(tiles[panel + 1], panel)
            ahead = spread_columns(tiles[panel + 1], panel + 1)
        for k in range(0, 8, 2):
            n = k + 1
            corner = spread_row(columns[k], k)
            side = spread_row(columns[n], k)
            other = spread_row(columns[n], n)
            first = 1.0 / corner
            second = corner * (1.0 / (corner * other - side * side))
            row_k = {m: spread_row(columns[m], k) * first for m in range(n, 8)}
            row_n = {
                m: (spread_row(columns[m], n) - side * row_k[m]) * second for m in range(n + 1, 8)
            }
            lead_k = jnp.where(sub == k, 0.0, columns[k])
            lead_n = jnp.where(sub == n, 0.0, columns[n] - lead_k * row_k[n])
            lead_n = jnp.where(sub == k, row_k[n], lead_n)
            for m in range(n + 1, 8):
                column = jnp.where(sub == k, row_k[m], columns[m] - lead_k * row_k[m])
                columns[m] = jnp.where(sub == n, row_n[m], column - lead_n * row_n[m])
            for lead, reciprocal, at in ((lead_k, first, k), (lead_n, second, n)):
                here = lane == 8 * panel + at
                scaled = jnp.where(here, 1.0, spread_row(tile, at)) * reciprocal
                cleared = jnp.where(here & (sub > at), 0.0, tile)
                tile = cleared - jnp.where(sub > at, lead, 0.0) * scaled
                full = jnp.where(sub == at, scaled, jnp.where(here, 0.0, full) - lead * scaled)
            if follows:
                below[n] = below[n] - below[k] * row_k[n]
                for m in range(n + 1, 8):
                    below[m] = below[m] - below[k] * row_k[m] - below[n] * row_n[m]
                scaled_k = below[k] * first
                scaled_n = below[n] * second
                for m in range(8):
                    ahead[m] = (
                        ahead[m]
                        - below[k] * spread_row(scaled_k, m)
                        - below[n] * spread_row(scaled_n, m)
                    )
        tiles[panel] = tile
        rows = [spread_row(full, k) for k in range(8)]
        for t in range(panel + 1, count):
            leads = spread_columns(tiles[t], panel)
            later = jnp.where((lane >= 8 * panel) & (lane < 8 * panel + 8), 0.0, tiles[t])
            for k in range(8):
                later = later - leads[k] * rows[k]
            tiles[t] = later
        if follows:
            columns = ahead
    inverse = []
    for t in range(size // 8):
        diagonal = lane == sub + 8 * t
        pivots = jnp.sum(jnp.where(diagonal, tiles[t], 0.0), axis=1, keepdims=True)
        unit = jnp.where(diagonal, 1.0, jnp.where(lane < sub + 8 * t, tiles[t], 0.0))
        inverse.append(unit / jnp.sqrt(pivots))
    return jnp.concatenate(inverse, axis=0)


def basis_kernel(
    total_rows, sums_ref, trial_ref, coupled_ref, sigma_ref, projected_ref, basis_ref
):
    size = sums_ref.shape[1]
    scale = 1.0 / total_rows
    overlap = sums_ref[0:size, :] * scale
    projected = sums_ref[size : 2 * size, :] * scale
    projected_ref[...] = projected
    square = sums_ref[2 * size : 3 * size, :] * scale
    row = lax.broadcasted_iota(jnp.int32, (size, size), 0)
    lane = lax.broadcasted_iota(jnp.int32, (size, size), 1)
    middle = jnp.where(row == lane, 2.0, 0.0) - overlap
    folded = jnp.dot(middle, projected, precision=HIGHEST, preferred_element_type=jnp.float32)
    gram = square - lax.dot_general(
        projected, folded, (((0,), (0,)), ((), ())),
        precision=HIGHEST, preferred_element_type=jnp.float32,
    )
    coupled = coupled_ref[...]
    sigma_ref[...] = coupled
    trial = trial_ref[...]
    residual = coupled.astype(jnp.float32)
    for term in split_three(projected):
        residual = residual - jnp.dot(trial, term, preferred_element_type=jnp.float32)
    upper = inverse_factor(gram).T
    basis_ref[...] = jnp.dot(
        residual, upper, precision=HIGHEST, preferred_element_type=jnp.float32
    )


def on_device(n_blk, n_col, trial, omega, table, block_type, cycle_offset, source_block):
    row_count, vec_count = trial.shape
    pair_block = table.shape[1]
    blocks = row_count // pair_block
    rows = 2 * vec_count
    near = max(size for size in (4, 2, 1) if n_blk % size == 0)
    group = near * n_col
    far = n_blk // near
    rows = 2 * vec_count
    piece = rows // group
    own_piece = vec_count // group
    vmem = pl.BlockSpec(memory_space=pltpu.VMEM)
    hbm = pl.BlockSpec(memory_space=pltpu.HBM)
    dma = pltpu.SemaphoreType.DMA
    coupled, sums = pl.pallas_call(
        functools.partial(couple_kernel, n_blk, n_col, near),
        out_shape=(
            jax.ShapeDtypeStruct((row_count, vec_count), jnp.bfloat16),
            jax.ShapeDtypeStruct((3 * vec_count, vec_count), jnp.float32),
        ),
        in_specs=[hbm] * 6,
        out_specs=(vmem, vmem),
        scratch_shapes=[
            pltpu.SMEM(block_type.shape, jnp.int32),
            pltpu.SMEM(block_type.shape, jnp.int32),
            pltpu.SMEM(block_type.shape, jnp.int32),
            pltpu.VMEM(table.shape, jnp.bfloat16),
            pltpu.VMEM(table.shape, jnp.bfloat16),
            pltpu.VMEM((2 * REACH + 1, blocks, pair_block // 2, vec_count), jnp.bfloat16),
            pltpu.VMEM((2 * REACH + 1, blocks, pair_block // 2, vec_count), jnp.bfloat16),
            pltpu.VMEM((blocks, pair_block, vec_count), jnp.bfloat16),
            pltpu.VMEM((vec_count, row_count), jnp.bfloat16),
            pltpu.VMEM((blocks, pair_block), jnp.float32),
            pltpu.VMEM((blocks, pair_block, vec_count), jnp.float32),
            pltpu.VMEM((vec_count, vec_count), jnp.float32),
            pltpu.VMEM((group - 1, own_piece, vec_count), jnp.float32),
            pltpu.VMEM((far, own_piece, vec_count), jnp.float32),
            pltpu.VMEM((vec_count, vec_count), jnp.float32),
            pltpu.VMEM((rows, vec_count), jnp.float32),
            pltpu.VMEM((group - 1, piece, vec_count), jnp.float32),
            pltpu.VMEM((far, piece, vec_count), jnp.float32),
            pltpu.VMEM((rows, vec_count), jnp.float32),
            dma((8,)),
            dma((8, PARTS)),
            dma((8, PARTS)),
            dma((group - 1,)),
            dma((group - 1,)),
            dma((far - 1,)),
            dma((far - 1,)),
            dma((group - 1,)),
            dma((group - 1,)),
            dma((group - 1,)),
            dma((group - 1,)),
            dma((far - 1,)),
            dma((far - 1,)),
            dma((group - 1,)),
            dma((group - 1,)),
        ],
        compiler_params=pltpu.CompilerParams(
            collective_id=0, has_side_effects=True, vmem_limit_bytes=24 << 20
        ),
        name="couple",
    )(
        *(
            pltpu.with_memory_space_constraint(operand, pltpu.HBM)
            for operand in (
                block_type,
                cycle_offset,
                source_block,
                trial.reshape(blocks, pair_block, vec_count),
                omega.reshape(blocks, pair_block),
                table,
            )
        )
    )
    sigma, projected, basis = pl.pallas_call(
        functools.partial(basis_kernel, row_count * n_blk * n_col),
        out_shape=(
            jax.ShapeDtypeStruct((row_count, vec_count), jnp.bfloat16),
            jax.ShapeDtypeStruct((vec_count, vec_count), jnp.float32),
            jax.ShapeDtypeStruct((row_count, vec_count), jnp.float32),
        ),
        in_specs=[vmem] * 3,
        out_specs=(vmem, vmem, vmem),
        compiler_params=pltpu.CompilerParams(vmem_limit_bytes=24 << 20),
        name="basis",
    )(sums, trial, coupled)
    return (sigma, projected, basis)


def solution(mesh):
    placed = (
        P(("blk", "col"), None),
        P(("blk", "col")),
        P(),
        P(("blk", "col"), None),
        P(("blk", "col"), None),
        P(("blk", "col"), None),
    )
    return jax.shard_map(
        functools.partial(on_device, mesh.shape["blk"], mesh.shape["col"]),
        mesh=mesh,
        in_specs=placed,
        out_specs=(P(("blk", "col"), None), P(), P(("blk", "col"), None)),
        check_vma=False,
    )
```
